512 devices in a mesh: cuts: 16 (over y, z_hi), slab: 32 (over x, z_lo, core).
Axes of the slice: x: 4, y: 8, z: 8 (z_hi: 2, z_lo: 4; z = z_hi * 4 + z_lo), core: 2. Of those that a mesh axis runs over, the one named last changes fastest.
Arguments:
- states: float32 [16, 64, 256, 128], P(None, 'slab', 'cuts'), may hold values from -4 to 4
- diffusivity: float32 [64, 256, 128], P('slab'), may hold values from 0.04 to 0.08
- coarse_gain: float32 [64, 256, 128], P('slab'), may hold values from 0.2 to 0.99
- read_block: int32 [16, 16, 2], replicated, may hold values from 0 to 63
- read_count: int32 [16, 16], replicated, may hold values from 0 to 2, as said below
Outputs:
- new_states: float32 [16, 64, 256, 128], P(None, 'slab', 'cuts')
- fetched_blocks: float32 [16, 16, 2, 64, 4, 128], P('cuts', None, None, 'slab')
The draws below stay inside these ranges and needn't reach their ends.
Inputs may be any that keep to these rules, and one draw needn't show every extreme that they name: `read_block`: block ids count in units of 4 y rows. Slots of read_block at or beyond read_count[d, s] are not read. In every draw some slice d reads 2 blocks from every slice.
All inputs are finite; a program needn't handle non-finite values.
Results may differ from the reference program's by a relative error of at most 0.00002.
Values sent between devices are 32-bit elements; how exact they have to be, the bound alone decides.
No kernel may reach another device: no remote copies, remote signals or barrier semaphores. Data moves between devices by JAX's collectives and lax.ppermute only.
A program may use at most 64 MiB of HBM per device.

```python
import jax
import jax.numpy as jnp
from jax import lax

NY = 256
NX = 128
FINE = 8
BY = 4
PAIR = 2
SLICES = 16
NZ = 64


def draw_states(key, part):
    shape = (SLICES, NZ, NY, NX)
    z_index = jnp.arange(NZ, dtype=jnp.int32)[:, None]
    y_index = jnp.arange(NY, dtype=jnp.int32)[None, :]
    parity = (z_index + y_index) % 2
    alternate = jnp.where(parity == 0, 1.0, -1.0).astype(jnp.float32)[None, :, :, None]
    noise = jax.random.normal(key, shape, jnp.float32)
    values = 2.0 * alternate + 0.8 * noise
    return jnp.clip(values, -4.0, 4.0)


def draw_diffusivity(key, part):
    shape = (NZ, NY, NX)
    exponent = jax.random.uniform(key, shape, jnp.float32, 0.0, 1.0)
    values = 0.04 * jnp.exp(exponent * jnp.log(2.0))
    return jnp.clip(values, 0.04, 0.08)


def draw_coarse_gain(key, part):
    shape = (NZ, NY, NX)
    first_key, second_key, third_key = jax.random.split(key, 3)
    slow_gain = jax.random.uniform(first_key, shape, jnp.float32, 0.88, 0.99)
    fast_gain = jax.random.uniform(second_key, shape, jnp.float32, 0.2, 0.6)
    share = 0.5
    chooser = jax.random.uniform(third_key, shape, jnp.float32)
    return jnp.where(chooser < share, slow_gain, fast_gain)


def draw_read_count(key, part):
    first_key, second_key = jax.random.split(jax.random.fold_in(key, 7))
    counts = jax.random.randint(first_key, (SLICES, SLICES), 0, PAIR + 1, dtype=jnp.int32)
    full_row = jax.random.randint(second_key, (), 0, SLICES, dtype=jnp.int32)
    row_index = jnp.arange(SLICES, dtype=jnp.int32)[:, None]
    return jnp.where(row_index == full_row, jnp.int32(PAIR), counts).astype(jnp.int32)


def place_ends(values, rng, smallest, high):
    dims = values.shape
    index_at = [jax.random.randint(jax.random.fold_in(rng, axis), (), 0, dims[axis]) for axis in range(len(dims))]
    values = values.at[tuple(index_at)].set(smallest)
    longest = dims.index(max(dims))
    index_at[longest] = (index_at[longest] + 1) % dims[longest]
    return values.at[tuple(index_at)].set(high)


def setup_inputs(seed: int = 0) -> dict:
    keys = jax.random.split(jax.random.key(seed), 6)
    states = draw_states(jax.random.fold_in(keys[5], 71), 0)
    diffusivity = draw_diffusivity(jax.random.fold_in(keys[5], 71), 0)
    coarse_gain = draw_coarse_gain(jax.random.fold_in(keys[5], 71), 0)
    read_block = place_ends(jax.random.randint(keys[3], (SLICES, SLICES, PAIR), 0, NY // BY), jax.random.fold_in(keys[3], 1), 0, (NY // BY) - 1).astype(jnp.int32)
    read_count = draw_read_count(jax.random.fold_in(keys[5], 71), 0)
    return dict(states=states, diffusivity=diffusivity, coarse_gain=coarse_gain, read_block=read_block, read_count=read_count)


courant = 0.45


def face_values(kappa_ext):
    face_z = 0.5 * (kappa_ext[1:] + kappa_ext[:-1])
    pad_y = jnp.pad(kappa_ext, ((0, 0), (1, 1), (0, 0)))
    face_y = 0.5 * (pad_y[:, 1:] + pad_y[:, :-1])
    pad_x = jnp.pad(kappa_ext, ((0, 0), (0, 0), (1, 1)))
    face_x = 0.5 * (pad_x[:, :, 1:] + pad_x[:, :, :-1])
    return face_z, face_y, face_x


def fine_step(field, face_z, face_y, face_x):
    centre = field[1:-1]
    upper_z = field[2:]
    lower_z = field[:-2]
    flux_sum = face_z[1:] * (upper_z - centre) + face_z[:-1] * (lower_z - centre)
    pad_y = jnp.pad(centre, ((0, 0), (1, 1), (0, 0)))
    faces_y = face_y[1:-1]
    flux_sum = flux_sum + faces_y[:, 1:] * (pad_y[:, 2:] - centre) + faces_y[:, :-1] * (pad_y[:, :-2] - centre)
    pad_x = jnp.pad(centre, ((0, 0), (0, 0), (1, 1)))
    faces_x = face_x[1:-1]
    flux_sum = flux_sum + faces_x[:, :, 1:] * (pad_x[:, :, 2:] - centre) + faces_x[:, :, :-1] * (pad_x[:, :, :-2] - centre)
    return centre + flux_sum - courant * (centre - lower_z)


def reference(states, diffusivity, coarse_gain, read_block, read_count):
    kappa_ext = jnp.pad(diffusivity, ((1, 1), (0, 0), (0, 0)))
    face_z, face_y, face_x = face_values(kappa_ext)

    def propagate(field):
        def single_step(step_index, current):
            return fine_step(jnp.pad(current, ((1, 1), (0, 0), (0, 0))), face_z, face_y, face_x)
        return lax.fori_loop(0, FINE, single_step, field)

    fine_end = lax.map(propagate, states)
    difference = fine_end - coarse_gain * states

    def advance(carried, change):
        updated = coarse_gain * carried + change
        return updated, updated

    unused, new_states = lax.scan(advance, states[0], difference)
    blocks = fine_end.reshape(SLICES, NZ, NY // BY, BY, NX).transpose(0, 2, 1, 3, 4)
    source = jnp.arange(SLICES, dtype=jnp.int32)[None, :, None]
    picked = blocks[source, read_block]
    live_slot = jnp.arange(PAIR, dtype=jnp.int32)[None, None, :] < read_count[:, :, None]
    fetched_blocks = jnp.where(live_slot[:, :, :, None, None, None], picked, jnp.zeros_like(picked))
    return new_states, fetched_blocks
```

```python
import functools

import jax
import jax.numpy as jnp
from jax import lax
from jax.experimental import pallas as pl
from jax.experimental.pallas import tpu as pltpu
from jax.sharding import Mesh
from jax.sharding import PartitionSpec as P

FINE = 8
BY = 4
COURANT = 0.45

RING = ("zh", "zl", "c")
NEAR = ("zl", "c")
SLAB = ("x", "zl", "c")
CUTS = ("y", "zh")

VMEM = pl.BlockSpec(memory_space=pltpu.VMEM)
SMEM = pl.BlockSpec(memory_space=pltpu.SMEM)
PARAMS = pltpu.CompilerParams(vmem_limit_bytes=40 * 2**20)


def fine_kernel(
    edge, own, low, high, kappa_in, out, u, kappa, c0, zp, zm, yp, ym, xp, xm
):
    depth, rows, lanes = u.shape

    def place(layer, first, second):
        u[layer, 8:24] = first[0:16]
        u[layer, 40:48] = first[16:24]
        u[layer, 24:40] = second[0:16]
        u[layer, 0:8] = second[16:24]

    for j in range(8):
        for k in range(2):
            place(8 + 2 * j + k, own[0, j, k], own[1, j, k])
            kappa[8 + 2 * j + k] = kappa_in[j, 0, k]
            if j >= 4:
                kappa[2 * (j - 4) + k] = kappa_in[j, 1, k]
            else:
                kappa[24 + 2 * j + k] = kappa_in[j, 1, k]
    for j in range(4):
        for k in range(2):
            place(2 * j + k, low[0, j, k], low[1, j, k])
            place(24 + 2 * j + k, high[0, j, k], high[1, j, k])

    row = lax.broadcasted_iota(jnp.int32, (rows, lanes), 0)
    lane = lax.broadcasted_iota(jnp.int32, (rows, lanes), 1)
    inside_y = jnp.where(
        row < 8, edge[0], jnp.where(row >= rows - 8, edge[1], 1)
    ).astype(jnp.float32)
    not_first = jnp.where(lane == 0, 0.0, 1.0)
    not_last = jnp.where(lane == lanes - 1, 0.0, 1.0)

    def coefficients(z, _):
        inside_z = jnp.where(z < 8, edge[2], jnp.where(z >= depth - 8, edge[3], 1))
        mask = inside_y * inside_z.astype(jnp.float32)
        here = kappa[z]
        up = 0.5 * (here + kappa[z + 1])
        down = 0.5 * (here + kappa[z - 1])
        north = 0.5 * (here + pltpu.roll(here, rows - 1, 0))
        south = 0.5 * (here + pltpu.roll(here, 1, 0))
        east = 0.5 * (here + pltpu.roll(here, lanes - 1, 1) * not_last)
        west = 0.5 * (here + pltpu.roll(here, 1, 1) * not_first)
        total = ((up + down) + (north + south)) + (east + west)
        c0[z] = ((1.0 - COURANT) - total) * mask
        zp[z] = up * mask
        zm[z] = (down + COURANT) * mask
        yp[z] = north * mask
        ym[z] = south * mask
        xp[z] = east * (mask * not_last)
        xm[z] = west * (mask * not_first)
        return 0

    lax.fori_loop(1, depth - 1, coefficients, 0)

    for step in range(1, FINE + 1):
        last = step == FINE

        def layer(z, carry):
            below, here = carry
            above = u[z + 1]
            new = (
                (c0[z] * here + zp[z] * above)
                + (zm[z] * below + yp[z] * pltpu.roll(here, rows - 1, 0))
                + (
                    ym[z] * pltpu.roll(here, 1, 0)
                    + xp[z] * pltpu.roll(here, lanes - 1, 1)
                )
                + xm[z] * pltpu.roll(here, 1, 1)
            )
            if last:
                out[z - 8] = new[8 : rows - 8]
            else:
                u[z] = new
            return here, above

        lax.fori_loop(step, depth - step, layer, (u[step - 1], u[step]), unroll=2)


def pick_kernel(blocks, counts, me, tiles, out):
    slices = out.shape[0]
    upper = lax.broadcasted_iota(jnp.int32, out.shape[2:], 0) >= BY
    for d in range(slices):
        count = counts[d * slices + me[0]]
        first = blocks[(d * slices + me[0]) * 2]
        second = blocks[(d * slices + me[0]) * 2 + 1]
        for k in range(2):
            def half(block, slot):
                start = pl.multiple_of(((block >> 1) & 3) * 8, 8)
                tile = tiles[(block >> 3) & 7, k, pl.ds(start, 8), :]
                turned = pltpu.roll(tile, BY, 0)
                fits = jnp.where((block & 1) == slot, 1, 0)
                live = jnp.where(slot < count, 1, 0)
                chosen = jnp.where(jnp.full(tile.shape, fits) == 1, tile, turned)
                return jnp.where(jnp.full(tile.shape, live) == 1, chosen, 0.0)

            out[d, k] = jnp.where(upper, half(second, 1), half(first, 0))


def pack_kernel(fine, picked, out):
    for h in range(2):
        for q in range(8):
            out[h, q, :, 0:16] = fine[2 * q : 2 * q + 2, 16 * h : 16 * h + 16]
            out[h, q, :, 16:24] = picked[q, h]


def advance_kernel(received, states, gain, new_states, fetched):
    factor = gain[...]
    carried = states[0]
    for s in range(received.shape[0]):
        fine = received[s, :, 0:16]
        change = fine - factor * states[s]
        carried = factor * carried + change
        new_states[s] = carried
        tile = received[s, :, 16:24]
        fetched[s, 0] = tile[:, 0:4]
        fetched[s, 1] = tile[:, 4:8]


def exchange(value, axes):
    return lax.all_to_all(value, axes, 0, 0, tiled=True)


def body(states, diffusivity, coarse_gain, read_block, read_count):
    f32 = jnp.float32
    slices, thick, own_rows, lanes = states.shape
    y, zh, x = lax.axis_index("y"), lax.axis_index("zh"), lax.axis_index("x")
    zl = lax.axis_index("zl")
    ny, nx = lax.axis_size("y"), lax.axis_size("x")
    me = lax.axis_index(RING)
    cut = lax.axis_index(CUTS)
    tile_rows = 2 * own_rows
    wide = tile_rows + 2 * FINE
    half = slices // 2

    edge_rows = jnp.where(zh == 1, states[:, :, own_rows - FINE :], states[:, :, :FINE])
    pairs = [(i, i + 2) for i in range(1, 2 * ny - 2, 2)]
    pairs += [(i, i - 2) for i in range(2, 2 * ny, 2)]
    side_rows = lax.ppermute(edge_rows, CUTS, pairs)

    padded = jnp.pad(diffusivity, ((0, 0), (FINE, FINE), (0, 0)))
    kappa = lax.dynamic_slice_in_dim(padded, y * tile_rows, wide, 1)
    near = [((i, j), (i + 1, j)) for i in range(nx - 1) for j in (2, 3)]
    near += [((i, j), (i - 1, j)) for i in range(1, nx) for j in (0, 1)]
    flat = [(a * 4 + b, c * 4 + d) for (a, b), (c, d) in near]
    side_kappa = lax.ppermute(kappa, ("x", "zl"), flat)

    block = jnp.concatenate([states, side_rows], axis=2)
    own = exchange(block, RING).reshape(2, half, thick, own_rows + FINE, lanes)
    kappas = lax.all_gather(jnp.stack([kappa, side_kappa]), NEAR)

    up = [(i, i + 1) for i in range(nx - 1)]
    down = [(i + 1, i) for i in range(nx - 1)]
    low = lax.ppermute(own[:, half // 2 :], "x", up)
    high = lax.ppermute(own[:, : half // 2], "x", down)

    edge = jnp.stack([y > 0, y < ny - 1, x > 0, x < nx - 1]).astype(jnp.int32)
    deep = half * thick
    region = (deep + 2 * FINE, wide, lanes)
    fine = pl.pallas_call(
        fine_kernel,
        out_shape=jax.ShapeDtypeStruct((deep, tile_rows, lanes), f32),
        in_specs=[SMEM, VMEM, VMEM, VMEM, VMEM],
        out_specs=VMEM,
        scratch_shapes=[pltpu.VMEM(region, f32)] * 9,
        compiler_params=PARAMS,
        name="fine",
    )(edge, own, low, high, kappas)

    tiles = exchange(fine.reshape(ny, deep // ny, tile_rows, lanes), "y")
    picked = pl.pallas_call(
        pick_kernel,
        out_shape=jax.ShapeDtypeStruct((slices, thick, 2 * BY, lanes), f32),
        in_specs=[SMEM, SMEM, SMEM, VMEM],
        out_specs=VMEM,
        compiler_params=PARAMS,
        name="pick",
    )(read_block.reshape(-1), read_count.reshape(-1), me[None], tiles)
    picked = exchange(picked, "y").reshape(ny, 2, thick, 2 * BY, lanes)
    payload = pl.pallas_call(
        pack_kernel,
        out_shape=jax.ShapeDtypeStruct(
            (2, half, thick, own_rows + 2 * BY, lanes), f32
        ),
        in_specs=[VMEM, VMEM],
        out_specs=VMEM,
        compiler_params=PARAMS,
        name="pack",
    )(fine, picked)
    received = exchange(
        payload.reshape(slices, thick, own_rows + 2 * BY, lanes), RING
    )
    gain = lax.dynamic_slice_in_dim(coarse_gain, cut * own_rows, own_rows, 1)
    new_states, fetched = pl.pallas_call(
        advance_kernel,
        out_shape=(
            jax.ShapeDtypeStruct(states.shape, f32),
            jax.ShapeDtypeStruct((slices, 2, thick, BY, lanes), f32),
        ),
        in_specs=[VMEM, VMEM, VMEM],
        out_specs=(VMEM, VMEM),
        compiler_params=PARAMS,
        name="advance",
    )(received, states, gain)
    return new_states, fetched[None]


def solution(mesh):
    grid = Mesh(mesh.devices.reshape(8, 2, 4, 4, 2), ("y", "zh", "x", "zl", "c"))
    placed = (P(None, SLAB, CUTS, None), P(SLAB, None, None), P(SLAB, None, None), P(), P())
    return jax.shard_map(
        body,
        mesh=grid,
        in_specs=placed,
        out_specs=(P(None, SLAB, CUTS, None), P(CUTS, None, None, SLAB, None, None)),
        check_vma=False,
    )
```

```python
import jax
import jax.numpy as jnp
from jax import lax
from jax.experimental import pallas as pl
from jax.experimental.pallas import tpu as pltpu
from jax.sharding import Mesh
from jax.sharding import PartitionSpec as P

FINE = 8
BY = 4
COURANT = 0.45

RING = ("zh", "zl", "c")
SLAB = ("x", "zl", "c")
CUTS = ("y", "zh")

VMEM = pl.BlockSpec(memory_space=pltpu.VMEM)
SMEM = pl.BlockSpec(memory_space=pltpu.SMEM)
PARAMS = pltpu.CompilerParams(vmem_limit_bytes=40 * 2**20)


def join_kernel(own, south, north, first, second):
    for out, start in ((first, 0), (second, 4)):
        for j in range(4):
            for k in range(2):
                layer = 2 * j + k
                out[layer, 0:8] = south[start + j, k]
                out[layer, 8:24] = own[0, start + j, k]
                out[layer, 24:40] = own[1, start + j, k]
                out[layer, 40:48] = north[start + j, k]


def coefficient_kernel(edge, mine, other, c0, zp, zm, yp, ym, xp, xm, kappa):
    depth, rows, lanes = kappa.shape
    core = edge[4]
    for part, source in ((core, mine), (1 - core, other)):
        for j in range(4):
            side = 4 * (j - 2) if j >= 2 else 24 + 4 * j
            for k in range(2):
                kappa[8 + 4 * j + 2 * part + k] = source[j, 0, k]
                kappa[side + 2 * part + k] = source[j, 1, k]

    row = lax.broadcasted_iota(jnp.int32, (rows, lanes), 0)
    lane = lax.broadcasted_iota(jnp.int32, (rows, lanes), 1)
    inside = jnp.where(
        row < 8, edge[0], jnp.where(row >= rows - 8, edge[1], 1)
    ).astype(jnp.float32)
    below = inside * edge[2].astype(jnp.float32)
    above = inside * edge[3].astype(jnp.float32)
    not_first = jnp.where(lane == 0, 0.0, 1.0)
    not_last = jnp.where(lane == lanes - 1, 0.0, 1.0)
    for z in range(1, depth - 1):
        mask = below if z < 8 else above if z >= depth - 8 else inside
        here = kappa[z]
        up = 0.5 * (here + kappa[z + 1])
        down = 0.5 * (here + kappa[z - 1])
        north = 0.5 * (here + pltpu.roll(here, rows - 1, 0))
        south = 0.5 * (here + pltpu.roll(here, 1, 0))
        east = 0.5 * (here + pltpu.roll(here, lanes - 1, 1) * not_last)
        west = 0.5 * (here + pltpu.roll(here, 1, 1) * not_first)
        total = ((up + down) + (north + south)) + (east + west)
        c0[z] = ((1.0 - COURANT) - total) * mask
        zp[z] = up * mask
        zm[z] = (down + COURANT) * mask
        yp[z] = north * mask
        ym[z] = south * mask
        xp[z] = east * (mask * not_last)
        xm[z] = west * (mask * not_first)


def fine_kernel(low, first, second, high, c0, zp, zm, yp, ym, xp, xm, out, ends, u):
    depth, rows, lanes = u.shape
    parts = (low, first, second, high)
    for step in range(1, FINE + 1):
        at = (lambda z: parts[z // 8][z % 8]) if step == 1 else (lambda z: u[z])
        below, here = at(step - 1), at(step)
        for z in range(step, depth - step):
            above = at(z + 1)
            new = (
                (c0[z] * here + zp[z] * above)
                + (zm[z] * below + yp[z] * pltpu.roll(here, rows - 1, 0))
                + (
                    ym[z] * pltpu.roll(here, 1, 0)
                    + xp[z] * pltpu.roll(here, lanes - 1, 1)
                )
                + xm[z] * pltpu.roll(here, 1, 1)
            )
            if step < FINE:
                u[z] = new
            else:
                q, k = (z - 8) // 2, z % 2
                out[q, k] = new[8 : rows - 8]
                ends[0, q, k] = new[8:24]
                ends[1, q, k] = new[24:40]
            below, here = here, above


def pick_kernel(blocks, counts, me, tiles, out):
    slices = out.shape[0]
    upper = lax.broadcasted_iota(jnp.int32, out.shape[2:], 0) >= BY
    for d in range(slices):
        count = counts[d * slices + me[0]]
        first = blocks[(d * slices + me[0]) * 2]
        second = blocks[(d * slices + me[0]) * 2 + 1]
        for k in range(2):
            def half(block, slot):
                start = pl.multiple_of(((block >> 1) & 3) * 8, 8)
                tile = tiles[(block >> 3) & 7, k, pl.ds(start, 8), :]
                turned = pltpu.roll(tile, BY, 0)
                fits = jnp.where((block & 1) == slot, 1, 0)
                live = jnp.where(slot < count, 1, 0)
                chosen = jnp.where(jnp.full(tile.shape, fits) == 1, tile, turned)
                return jnp.where(jnp.full(tile.shape, live) == 1, chosen, 0.0)

            out[d, k] = jnp.where(upper, half(second, 1), half(first, 0))


def pack_kernel(ends, picked, out):
    for h in range(2):
        for q in range(8):
            out[h, q, :, 0:16] = ends[h, q]
            out[h, q, :, 16:24] = picked[q, h]


def advance_kernel(received, states, gain, new_states, fetched):
    factor = gain[...]
    carried = states[0]
    for s in range(received.shape[0]):
        fine = received[s, :, 0:16]
        change = fine - factor * states[s]
        carried = factor * carried + change
        new_states[s] = carried
        tile = received[s, :, 16:24]
        fetched[s, 0] = tile[:, 0:4]
        fetched[s, 1] = tile[:, 4:8]


def exchange(value, axes):
    return lax.all_to_all(value, axes, 0, 0, tiled=True)


def call(kernel, name, shapes, kinds, scratch=(), **more):
    outs = [jax.ShapeDtypeStruct(shape, jnp.float32) for shape in shapes]
    return pl.pallas_call(
        kernel,
        out_shape=outs,
        in_specs=kinds,
        out_specs=[VMEM] * len(outs),
        scratch_shapes=[pltpu.VMEM(shape, jnp.float32) for shape in scratch],
        compiler_params=PARAMS,
        name=name,
        **more,
    )


def body(states, diffusivity, coarse_gain, read_block, read_count):
    slices, thick, own_rows, lanes = states.shape
    y, x, c = lax.axis_index("y"), lax.axis_index("x"), lax.axis_index("c")
    ny, nx = lax.axis_size("y"), lax.axis_size("x")
    me = lax.axis_index(RING)
    cut = lax.axis_index(CUTS)
    tile_rows = 2 * own_rows
    wide = tile_rows + 2 * FINE
    half = slices // 2
    y_up = [(i, i + 1) for i in range(ny - 1)]
    y_down = [(i + 1, i) for i in range(ny - 1)]
    x_up = [(i, i + 1) for i in range(nx - 1)]
    x_down = [(i + 1, i) for i in range(nx - 1)]

    padded = jnp.pad(diffusivity, ((0, 0), (FINE, FINE), (0, 0)))
    kappa = lax.dynamic_slice_in_dim(padded, y * tile_rows, wide, 1)
    near = [((i, j), (i + 1, j)) for i in range(nx - 1) for j in (2, 3)]
    near += [((i, j), (i - 1, j)) for i in range(1, nx) for j in (0, 1)]
    flat = [(p * 4 + q, r * 4 + s) for (p, q), (r, s) in near]
    side_kappa = lax.ppermute(kappa, ("x", "zl"), flat)
    mine = lax.all_gather(jnp.stack([kappa, side_kappa]), "zl")

    own = exchange(states, RING).reshape(2, half, thick, own_rows, lanes)
    own, mine = lax.optimization_barrier((own, mine))
    other = lax.ppermute(mine, "c", [(0, 1), (1, 0)])
    south = lax.ppermute(own[1, :, :, own_rows - FINE :], "y", y_up)
    north = lax.ppermute(own[0, :, :, :FINE], "y", y_down)
    part = (FINE, wide, lanes)
    first, second = call(join_kernel, "join", [part] * 2, [VMEM] * 3)(own, south, north)
    low = lax.ppermute(second, "x", x_up)
    high = lax.ppermute(first, "x", x_down)

    edge = jnp.stack([y > 0, y < ny - 1, x > 0, x < nx - 1, c > 0]).astype(jnp.int32)
    deep = half * thick
    region = (deep + 2 * FINE, wide, lanes)
    coefficients = call(
        coefficient_kernel, "coefficients", [region] * 7, [SMEM, VMEM, VMEM], [region]
    )(edge, mine, other)
    fine, ends = call(
        fine_kernel,
        "fine",
        [(ny, deep // ny, tile_rows, lanes), (2, half, thick, own_rows, lanes)],
        [VMEM] * 11,
        [region],
    )(low, first, second, high, *coefficients)

    tiles = exchange(fine, "y")
    (picked,) = call(
        pick_kernel,
        "pick",
        [(slices, thick, 2 * BY, lanes)],
        [SMEM, SMEM, SMEM, VMEM],
    )(read_block.reshape(-1), read_count.reshape(-1), me[None], tiles)
    picked = exchange(picked, "y").reshape(ny, 2, thick, 2 * BY, lanes)
    (payload,) = call(
        pack_kernel, "pack", [(2, half, thick, own_rows + 2 * BY, lanes)], [VMEM] * 2
    )(ends, picked)
    received = exchange(
        payload.reshape(slices, thick, own_rows + 2 * BY, lanes), RING
    )
    gain = lax.dynamic_slice_in_dim(coarse_gain, cut * own_rows, own_rows, 1)
    new_states, fetched = call(
        advance_kernel,
        "advance",
        [states.shape, (slices, 2, thick, BY, lanes)],
        [VMEM] * 3,
    )(received, states, gain)
    return new_states, fetched[None]


def solution(mesh):
    grid = Mesh(mesh.devices.reshape(8, 2, 4, 4, 2), ("y", "zh", "x", "zl", "c"))
    placed = (P(None, SLAB, CUTS, None), P(SLAB, None, None), P(SLAB, None, None), P(), P())
    return jax.shard_map(
        body,
        mesh=grid,
        in_specs=placed,
        out_specs=(P(None, SLAB, CUTS, None), P(CUTS, None, None, SLAB, None, None)),
        check_vma=False,
    )
```

```python
import jax
import jax.numpy as jnp
from jax import lax
from jax.experimental import pallas as pl
from jax.experimental.pallas import tpu as pltpu
from jax.sharding import Mesh
from jax.sharding import PartitionSpec as P

FINE = 8
BY = 4
COURANT = 0.45

RING = ("zh", "zl", "c")
SLAB = ("x", "zl", "c")
CUTS = ("y", "zh")
CHIPS = ("zh", "zl")
RING_OFFSETS = (0, -1, 1, -2)

VMEM = pl.BlockSpec(memory_space=pltpu.VMEM)
SMEM = pl.BlockSpec(memory_space=pltpu.SMEM)
PARAMS = pltpu.CompilerParams(vmem_limit_bytes=40 * 2**20)


def join_kernel(own, south, north, first, second):
    for out, start in ((first, 0), (second, 4)):
        for j in range(4):
            for k in range(2):
                layer = 2 * j + k
                out[layer, 0:8] = south[start + j, k]
                out[layer, 8:24] = own[0, start + j, k]
                out[layer, 24:40] = own[1, start + j, k]
                out[layer, 40:48] = north[start + j, k]


def coefficient_kernel(edge, mine, other, c0, zp, zm, yp, ym, xp, xm, kappa):
    depth, rows, lanes = kappa.shape
    core = edge[4]
    for part, source in ((core, mine), (1 - core, other)):
        for i, offset in enumerate(RING_OFFSETS):
            j = (edge[5] + offset) & 3
            side = jnp.where(j >= 2, 4 * (j - 2), 24 + 4 * j)
            for k in range(2):
                kappa[8 + 4 * j + 2 * part + k] = source[i, 0, k]
                kappa[side + 2 * part + k] = source[i, 1, k]

    row = lax.broadcasted_iota(jnp.int32, (rows, lanes), 0)
    lane = lax.broadcasted_iota(jnp.int32, (rows, lanes), 1)
    inside = jnp.where(
        row < 8, edge[0], jnp.where(row >= rows - 8, edge[1], 1)
    ).astype(jnp.float32)
    below = inside * edge[2].astype(jnp.float32)
    above = inside * edge[3].astype(jnp.float32)
    not_first = jnp.where(lane == 0, 0.0, 1.0)
    not_last = jnp.where(lane == lanes - 1, 0.0, 1.0)
    for z in range(1, depth - 1):
        mask = below if z < 8 else above if z >= depth - 8 else inside
        here = kappa[z]
        up = 0.5 * (here + kappa[z + 1])
        down = 0.5 * (here + kappa[z - 1])
        north = 0.5 * (here + pltpu.roll(here, rows - 1, 0))
        south = 0.5 * (here + pltpu.roll(here, 1, 0))
        east = 0.5 * (here + pltpu.roll(here, lanes - 1, 1) * not_last)
        west = 0.5 * (here + pltpu.roll(here, 1, 1) * not_first)
        total = ((up + down) + (north + south)) + (east + west)
        c0[z] = ((1.0 - COURANT) - total) * mask
        zp[z] = up * mask
        zm[z] = (down + COURANT) * mask
        yp[z] = north * mask
        ym[z] = south * mask
        xp[z] = east * (mask * not_last)
        xm[z] = west * (mask * not_first)


def fine_kernel(low, first, second, high, c0, zp, zm, yp, ym, xp, xm, out, ends, u):
    depth, rows, lanes = u.shape
    parts = (low, first, second, high)
    for step in range(1, FINE + 1):
        at = (lambda z: parts[z // 8][z % 8]) if step == 1 else (lambda z: u[z])
        below, here = at(step - 1), at(step)
        for z in range(step, depth - step):
            above = at(z + 1)
            new = (
                (c0[z] * here + zp[z] * above)
                + (zm[z] * below + yp[z] * pltpu.roll(here, rows - 1, 0))
                + (
                    ym[z] * pltpu.roll(here, 1, 0)
                    + xp[z] * pltpu.roll(here, lanes - 1, 1)
                )
                + xm[z] * pltpu.roll(here, 1, 1)
            )
            if step < FINE:
                u[z] = new
            else:
                q, k = (z - 8) // 2, z % 2
                out[q, k] = new[8 : rows - 8]
                ends[0, q, k] = new[8:24]
                ends[1, q, k] = new[24:40]
            below, here = here, above


def pick_kernel(blocks, counts, me, tiles, out):
    slices = out.shape[0]
    upper = lax.broadcasted_iota(jnp.int32, out.shape[2:], 0) >= BY
    for d in range(slices):
        count = counts[d * slices + me[0]]
        first = blocks[(d * slices + me[0]) * 2]
        second = blocks[(d * slices + me[0]) * 2 + 1]
        for k in range(2):
            def half(block, slot):
                start = pl.multiple_of(((block >> 1) & 3) * 8, 8)
                tile = tiles[(block >> 3) & 7, k, pl.ds(start, 8), :]
                turned = pltpu.roll(tile, BY, 0)
                fits = jnp.where((block & 1) == slot, 1, 0)
                live = jnp.where(slot < count, 1, 0)
                chosen = jnp.where(jnp.full(tile.shape, fits) == 1, tile, turned)
                return jnp.where(jnp.full(tile.shape, live) == 1, chosen, 0.0)

            out[d, k] = jnp.where(upper, half(second, 1), half(first, 0))


def pack_kernel(ends, picked, out):
    for h in range(2):
        for q in range(8):
            out[h, q, :, 0:16] = ends[h, q]
            out[h, q, :, 16:24] = picked[q, h]


def advance_kernel(received, states, gain, new_states, fetched):
    factor = gain[...]
    carried = states[0]
    for s in range(received.shape[0]):
        fine = received[s, :, 0:16]
        change = fine - factor * states[s]
        carried = factor * carried + change
        new_states[s] = carried
        tile = received[s, :, 16:24]
        fetched[s, 0] = tile[:, 0:4]
        fetched[s, 1] = tile[:, 4:8]


def exchange(value, axes):
    return lax.all_to_all(value, axes, 0, 0, tiled=True)


def call(kernel, name, shapes, kinds, scratch=(), **more):
    outs = [jax.ShapeDtypeStruct(shape, jnp.float32) for shape in shapes]
    return pl.pallas_call(
        kernel,
        out_shape=outs,
        in_specs=kinds,
        out_specs=[VMEM] * len(outs),
        scratch_shapes=[pltpu.VMEM(shape, jnp.float32) for shape in scratch],
        compiler_params=PARAMS,
        name=name,
        **more,
    )


def body(states, diffusivity, coarse_gain, read_block, read_count):
    slices, thick, own_rows, lanes = states.shape
    y, x, c = lax.axis_index("y"), lax.axis_index("x"), lax.axis_index("c")
    ny, nx = lax.axis_size("y"), lax.axis_size("x")
    me = lax.axis_index(RING)
    cut = lax.axis_index(CUTS)
    tile_rows = 2 * own_rows
    wide = tile_rows + 2 * FINE
    half = slices // 2
    y_up = [(i, i + 1) for i in range(ny - 1)]
    y_down = [(i + 1, i) for i in range(ny - 1)]
    x_up = [(i, i + 1) for i in range(nx - 1)]
    x_down = [(i + 1, i) for i in range(nx - 1)]

    padded = jnp.pad(diffusivity, ((0, 0), (FINE, FINE), (0, 0)))
    kappa = lax.dynamic_slice_in_dim(padded, y * tile_rows, wide, 1)
    near = [((i, j), (i + 1, j)) for i in range(nx - 1) for j in (2, 3)]
    near += [((i, j), (i - 1, j)) for i in range(1, nx) for j in (0, 1)]
    flat = [(p * 4 + q, r * 4 + s) for (p, q), (r, s) in near]
    side_kappa = lax.ppermute(kappa, ("x", "zl"), flat)
    pieces = jnp.stack([kappa, side_kappa])
    around = lax.axis_size(CHIPS)
    mine = jnp.stack(
        [pieces]
        + [
            lax.ppermute(
                pieces, CHIPS, [(i, (i - offset) % around) for i in range(around)]
            )
            for offset in RING_OFFSETS[1:]
        ]
    )

    own = exchange(states, RING).reshape(2, half, thick, own_rows, lanes)
    other = lax.ppermute(mine, "c", [(0, 1), (1, 0)])
    south = lax.ppermute(own[1, :, :, own_rows - FINE :], "y", y_up)
    north = lax.ppermute(own[0, :, :, :FINE], "y", y_down)
    part = (FINE, wide, lanes)
    first, second = call(join_kernel, "join", [part] * 2, [VMEM] * 3)(own, south, north)
    low = lax.ppermute(second, "x", x_up)
    high = lax.ppermute(first, "x", x_down)

    flags = [y > 0, y < ny - 1, x > 0, x < nx - 1, c, lax.axis_index("zl")]
    edge = jnp.stack([flag.astype(jnp.int32) for flag in flags])
    deep = half * thick
    region = (deep + 2 * FINE, wide, lanes)
    coefficients = call(
        coefficient_kernel, "coefficients", [region] * 7, [SMEM, VMEM, VMEM], [region]
    )(edge, mine, other)
    fine, ends = call(
        fine_kernel,
        "fine",
        [(ny, deep // ny, tile_rows, lanes), (2, half, thick, own_rows, lanes)],
        [VMEM] * 11,
        [region],
    )(low, first, second, high, *coefficients)

    tiles = exchange(fine, "y")
    (picked,) = call(
        pick_kernel,
        "pick",
        [(slices, thick, 2 * BY, lanes)],
        [SMEM, SMEM, SMEM, VMEM],
    )(read_block.reshape(-1), read_count.reshape(-1), me[None], tiles)
    picked = exchange(picked, "y").reshape(ny, 2, thick, 2 * BY, lanes)
    (payload,) = call(
        pack_kernel, "pack", [(2, half, thick, own_rows + 2 * BY, lanes)], [VMEM] * 2
    )(ends, picked)
    received = exchange(
        payload.reshape(slices, thick, own_rows + 2 * BY, lanes), RING
    )
    gain = lax.dynamic_slice_in_dim(coarse_gain, cut * own_rows, own_rows, 1)
    new_states, fetched = call(
        advance_kernel,
        "advance",
        [states.shape, (slices, 2, thick, BY, lanes)],
        [VMEM] * 3,
    )(received, states, gain)
    return new_states, fetched[None]


def solution(mesh):
    grid = Mesh(mesh.devices.reshape(8, 2, 4, 4, 2), ("y", "zh", "x", "zl", "c"))
    placed = (P(None, SLAB, CUTS, None), P(SLAB, None, None), P(SLAB, None, None), P(), P())
    return jax.shard_map(
        body,
        mesh=grid,
        in_specs=placed,
        out_specs=(P(None, SLAB, CUTS, None), P(CUTS, None, None, SLAB, None, None)),
        check_vma=False,
    )
```

```python
import jax
import jax.numpy as jnp
from jax import lax
from jax.experimental import pallas as pl
from jax.experimental.pallas import tpu as pltpu
from jax.sharding import Mesh
from jax.sharding import PartitionSpec as P

FINE = 8
BY = 4
COURANT = 0.45

RING = ("zh", "zl", "c")
SLAB = ("x", "zl", "c")
CUTS = ("y", "zh")
CHIPS = ("zh", "zl")
RING_OFFSETS = (0, -1, 1, -2)

VMEM = pl.BlockSpec(memory_space=pltpu.VMEM)
SMEM = pl.BlockSpec(memory_space=pltpu.SMEM)
PARAMS = pltpu.CompilerParams(vmem_limit_bytes=40 * 2**20)


def coefficient_kernel(edge, mine, other, c0, zp, zm, yp, ym, xp, xm, kappa):
    depth, rows, lanes = kappa.shape
    core = edge[4]
    for part, source in ((core, mine), (1 - core, other)):
        for i, offset in enumerate(RING_OFFSETS):
            j = (edge[5] + offset) & 3
            side = jnp.where(j >= 2, 4 * (j - 2), 24 + 4 * j)
            for k in range(2):
                kappa[8 + 4 * j + 2 * part + k] = source[i, 0, k]
                kappa[side + 2 * part + k] = source[i, 1, k]

    row = lax.broadcasted_iota(jnp.int32, (rows, lanes), 0)
    lane = lax.broadcasted_iota(jnp.int32, (rows, lanes), 1)
    inside = jnp.where(
        row < 8, edge[0], jnp.where(row >= rows - 8, edge[1], 1)
    ).astype(jnp.float32)
    below = inside * edge[2].astype(jnp.float32)
    above = inside * edge[3].astype(jnp.float32)
    not_first = jnp.where(lane == 0, 0.0, 1.0)
    not_last = jnp.where(lane == lanes - 1, 0.0, 1.0)
    for z in range(1, depth - 1):
        mask = below if z < 8 else above if z >= depth - 8 else inside
        here = kappa[z]
        up = 0.5 * (here + kappa[z + 1])
        down = 0.5 * (here + kappa[z - 1])
        north = 0.5 * (here + pltpu.roll(here, rows - 1, 0))
        south = 0.5 * (here + pltpu.roll(here, 1, 0))
        east = 0.5 * (here + pltpu.roll(here, lanes - 1, 1) * not_last)
        west = 0.5 * (here + pltpu.roll(here, 1, 1) * not_first)
        total = ((up + down) + (north + south)) + (east + west)
        c0[z] = ((1.0 - COURANT) - total) * mask
        zp[z] = up * mask
        zm[z] = (down + COURANT) * mask
        yp[z] = north * mask
        ym[z] = south * mask
        xp[z] = east * (mask * not_last)
        xm[z] = west * (mask * not_first)


def fine_kernel(low, own, high, c0, zp, zm, yp, ym, xp, xm, out, ends, u):
    depth, rows, lanes = u.shape

    def given(z):
        part, layer = (low, z) if z < 8 else (own, z - 8) if z < 24 else (high, z - 24)
        near, far = part[0, layer // 2, layer % 2], part[1, layer // 2, layer % 2]
        return jnp.concatenate([far[16:24], near[0:16], far[0:16], near[16:24]])

    for step in range(1, FINE + 1):
        at = given if step == 1 else (lambda z: u[z])
        below, here = at(step - 1), at(step)
        for z in range(step, depth - step):
            above = at(z + 1)
            new = (
                (c0[z] * here + zp[z] * above)
                + (zm[z] * below + yp[z] * pltpu.roll(here, rows - 1, 0))
                + (
                    ym[z] * pltpu.roll(here, 1, 0)
                    + xp[z] * pltpu.roll(here, lanes - 1, 1)
                )
                + xm[z] * pltpu.roll(here, 1, 1)
            )
            if step < FINE:
                u[z] = new
            else:
                q, k = (z - 8) // 2, z % 2
                out[q, k] = new[8 : rows - 8]
                ends[0, q, k] = new[8:24]
                ends[1, q, k] = new[24:40]
            below, here = here, above


def pick_kernel(blocks, counts, me, tiles, out):
    slices = out.shape[0]
    upper = lax.broadcasted_iota(jnp.int32, out.shape[2:], 0) >= BY
    for d in range(slices):
        count = counts[d * slices + me[0]]
        first = blocks[(d * slices + me[0]) * 2]
        second = blocks[(d * slices + me[0]) * 2 + 1]
        for k in range(2):
            def half(block, slot):
                start = pl.multiple_of(((block >> 1) & 3) * 8, 8)
                tile = tiles[(block >> 3) & 7, k, pl.ds(start, 8), :]
                turned = pltpu.roll(tile, BY, 0)
                fits = jnp.where((block & 1) == slot, 1, 0)
                live = jnp.where(slot < count, 1, 0)
                chosen = jnp.where(jnp.full(tile.shape, fits) == 1, tile, turned)
                return jnp.where(jnp.full(tile.shape, live) == 1, chosen, 0.0)

            out[d, k] = jnp.where(upper, half(second, 1), half(first, 0))


def pack_kernel(ends, picked, out):
    for h in range(2):
        for q in range(8):
            out[h, q, :, 0:16] = ends[h, q]
            out[h, q, :, 16:24] = picked[q, h]


def advance_kernel(received, states, gain, new_states, fetched):
    factor = gain[...]
    carried = states[0]
    for s in range(received.shape[0]):
        fine = received[s, :, 0:16]
        change = fine - factor * states[s]
        carried = factor * carried + change
        new_states[s] = carried
        tile = received[s, :, 16:24]
        fetched[s, 0] = tile[:, 0:4]
        fetched[s, 1] = tile[:, 4:8]


def exchange(value, axes):
    return lax.all_to_all(value, axes, 0, 0, tiled=True)


def call(kernel, name, shapes, kinds, scratch=(), **more):
    outs = [jax.ShapeDtypeStruct(shape, jnp.float32) for shape in shapes]
    return pl.pallas_call(
        kernel,
        out_shape=outs,
        in_specs=kinds,
        out_specs=[VMEM] * len(outs),
        scratch_shapes=[pltpu.VMEM(shape, jnp.float32) for shape in scratch],
        compiler_params=PARAMS,
        name=name,
        **more,
    )


def body(states, diffusivity, coarse_gain, read_block, read_count):
    slices, thick, own_rows, lanes = states.shape
    y, zh = lax.axis_index("y"), lax.axis_index("zh")
    x, c = lax.axis_index("x"), lax.axis_index("c")
    ny, nx = lax.axis_size("y"), lax.axis_size("x")
    me = lax.axis_index(RING)
    cut = lax.axis_index(CUTS)
    tile_rows = 2 * own_rows
    wide = tile_rows + 2 * FINE
    half = slices // 2
    x_up = [(i, i + 1) for i in range(nx - 1)]
    x_down = [(i + 1, i) for i in range(nx - 1)]

    edge_rows = jnp.where(zh == 1, states[:, :, own_rows - FINE :], states[:, :, :FINE])
    pairs = [(i, i + 2) for i in range(1, 2 * ny - 2, 2)]
    pairs += [(i, i - 2) for i in range(2, 2 * ny, 2)]
    side_rows = lax.ppermute(edge_rows, CUTS, pairs)

    padded = jnp.pad(diffusivity, ((0, 0), (FINE, FINE), (0, 0)))
    kappa = lax.dynamic_slice_in_dim(padded, y * tile_rows, wide, 1)
    near = [((i, j), (i + 1, j)) for i in range(nx - 1) for j in (2, 3)]
    near += [((i, j), (i - 1, j)) for i in range(1, nx) for j in (0, 1)]
    flat = [(p * 4 + q, r * 4 + s) for (p, q), (r, s) in near]
    side_kappa = lax.ppermute(kappa, ("x", "zl"), flat)

    block = jnp.concatenate([states, side_rows], axis=2)
    pieces = jnp.stack([kappa, side_kappa])
    block, pieces = lax.optimization_barrier((block, pieces))
    own = exchange(block, RING).reshape(2, half, thick, own_rows + FINE, lanes)
    around = lax.axis_size(CHIPS)
    ring = [
        lax.ppermute(pieces, CHIPS, [(i, (i - offset) % around) for i in range(around)])
        for offset in RING_OFFSETS[1:]
    ]
    lower, upper = own[:, : half // 2], own[:, half // 2 :]
    lower, upper, *ring = lax.optimization_barrier((lower, upper, *ring))
    low = lax.ppermute(upper, "x", x_up)
    high = lax.ppermute(lower, "x", x_down)
    mine = jnp.stack([pieces, *ring])
    other = lax.ppermute(mine, "c", [(0, 1), (1, 0)])

    flags = [y > 0, y < ny - 1, x > 0, x < nx - 1, c, lax.axis_index("zl")]
    edge = jnp.stack([flag.astype(jnp.int32) for flag in flags])
    deep = half * thick
    region = (deep + 2 * FINE, wide, lanes)
    coefficients = call(
        coefficient_kernel, "coefficients", [region] * 7, [SMEM, VMEM, VMEM], [region]
    )(edge, mine, other)
    fine, ends = call(
        fine_kernel,
        "fine",
        [(ny, deep // ny, tile_rows, lanes), (2, half, thick, own_rows, lanes)],
        [VMEM] * 10,
        [region],
    )(low, own, high, *coefficients)

    tiles = exchange(fine, "y")
    (picked,) = call(
        pick_kernel,
        "pick",
        [(slices, thick, 2 * BY, lanes)],
        [SMEM, SMEM, SMEM, VMEM],
    )(read_block.reshape(-1), read_count.reshape(-1), me[None], tiles)
    picked = exchange(picked, "y").reshape(ny, 2, thick, 2 * BY, lanes)
    (payload,) = call(
        pack_kernel, "pack", [(2, half, thick, own_rows + 2 * BY, lanes)], [VMEM] * 2
    )(ends, picked)
    received = exchange(
        payload.reshape(slices, thick, own_rows + 2 * BY, lanes), RING
    )
    gain = lax.dynamic_slice_in_dim(coarse_gain, cut * own_rows, own_rows, 1)
    new_states, fetched = call(
        advance_kernel,
        "advance",
        [states.shape, (slices, 2, thick, BY, lanes)],
        [VMEM] * 3,
    )(received, states, gain)
    return new_states, fetched[None]


def solution(mesh):
    grid = Mesh(mesh.devices.reshape(8, 2, 4, 4, 2), ("y", "zh", "x", "zl", "c"))
    placed = (P(None, SLAB, CUTS, None), P(SLAB, None, None), P(SLAB, None, None), P(), P())
    return jax.shard_map(
        body,
        mesh=grid,
        in_specs=placed,
        out_specs=(P(None, SLAB, CUTS, None), P(CUTS, None, None, SLAB, None, None)),
        check_vma=False,
    )
```

```python
import jax
import jax.numpy as jnp
from jax import lax
from jax.experimental import pallas as pl
from jax.experimental.pallas import tpu as pltpu
from jax.sharding import Mesh
from jax.sharding import PartitionSpec as P

FINE = 8
BY = 4
COURANT = 0.45

RING = ("zh", "zl", "c")
SLAB = ("x", "zl", "c")
CUTS = ("y", "zh")
CHIPS = ("zh", "zl")
RING_OFFSETS = (0, -1, 1, -2)

VMEM = pl.BlockSpec(memory_space=pltpu.VMEM)
SMEM = pl.BlockSpec(memory_space=pltpu.SMEM)
PARAMS = pltpu.CompilerParams(vmem_limit_bytes=40 * 2**20)


def gather_kernel(place, mine, other, first, second, kappa):
    for part, source in ((place[0], mine), (1 - place[0], other)):
        for i, offset in enumerate(RING_OFFSETS):
            j = (place[1] + offset) & 3
            for k in range(2):
                kappa[4 * j + 2 * part + k] = source[i, k]
    for z in range(FINE):
        first[z] = kappa[z]
        second[z] = kappa[FINE + z]


def coefficient_kernel(
    edge, low, first, second, high, c0, zp, zm, yp, ym, xp, xm
):
    depth, rows, lanes = c0.shape
    parts = (low, first, second, high)
    at = lambda z: parts[z // 8][z % 8]
    row = lax.broadcasted_iota(jnp.int32, (rows, lanes), 0)
    lane = lax.broadcasted_iota(jnp.int32, (rows, lanes), 1)
    inside = jnp.where(
        row < 8, edge[0], jnp.where(row >= rows - 8, edge[1], 1)
    ).astype(jnp.float32)
    below = inside * edge[2].astype(jnp.float32)
    above = inside * edge[3].astype(jnp.float32)
    not_first = jnp.where(lane == 0, 0.0, 1.0)
    not_last = jnp.where(lane == lanes - 1, 0.0, 1.0)
    down, here = 0.5 * (at(0) + at(1)), at(1)
    for z in range(1, depth - 1):
        mask = below if z < 8 else above if z >= depth - 8 else inside
        after = at(z + 1)
        up = 0.5 * (here + after)
        north = 0.5 * (here + pltpu.roll(here, rows - 1, 0))
        south = 0.5 * (here + pltpu.roll(here, 1, 0))
        east = 0.5 * (here + pltpu.roll(here, lanes - 1, 1) * not_last)
        west = 0.5 * (here + pltpu.roll(here, 1, 1) * not_first)
        total = ((up + down) + (north + south)) + (east + west)
        c0[z] = ((1.0 - COURANT) - total) * mask
        zp[z] = up * mask
        zm[z] = (down + COURANT) * mask
        yp[z] = north * mask
        ym[z] = south * mask
        xp[z] = east * (mask * not_last)
        xm[z] = west * (mask * not_first)
        down, here = up, after


def fine_kernel(low, own, high, c0, zp, zm, yp, ym, xp, xm, out, ends, u):
    depth, rows, lanes = u.shape

    def given(z):
        part, layer = (low, z) if z < 8 else (own, z - 8) if z < 24 else (high, z - 24)
        near, far = part[0, layer // 2, layer % 2], part[1, layer // 2, layer % 2]
        return jnp.concatenate([far[16:24], near[0:16], far[0:16], near[16:24]])

    for step in range(1, FINE + 1):
        at = given if step == 1 else (lambda z: u[z])
        below, here = at(step - 1), at(step)
        for z in range(step, depth - step):
            above = at(z + 1)
            new = (
                (c0[z] * here + zp[z] * above)
                + (zm[z] * below + yp[z] * pltpu.roll(here, rows - 1, 0))
                + (
                    ym[z] * pltpu.roll(here, 1, 0)
                    + xp[z] * pltpu.roll(here, lanes - 1, 1)
                )
                + xm[z] * pltpu.roll(here, 1, 1)
            )
            if step < FINE:
                u[z] = new
            else:
                q, k = (z - 8) // 2, z % 2
                out[q, k] = new[8 : rows - 8]
                ends[0, q, k] = new[8:24]
                ends[1, q, k] = new[24:40]
            below, here = here, above


def pick_kernel(blocks, counts, me, tiles, out):
    slices = out.shape[0]
    upper = lax.broadcasted_iota(jnp.int32, out.shape[2:], 0) >= BY
    for d in range(slices):
        count = counts[d * slices + me[0]]
        first = blocks[(d * slices + me[0]) * 2]
        second = blocks[(d * slices + me[0]) * 2 + 1]
        for k in range(2):
            def half(block, slot):
                start = pl.multiple_of(((block >> 1) & 3) * 8, 8)
                tile = tiles[(block >> 3) & 7, k, pl.ds(start, 8), :]
                turned = pltpu.roll(tile, BY, 0)
                fits = jnp.where((block & 1) == slot, 1, 0)
                live = jnp.where(slot < count, 1, 0)
                chosen = jnp.where(jnp.full(tile.shape, fits) == 1, tile, turned)
                return jnp.where(jnp.full(tile.shape, live) == 1, chosen, 0.0)

            out[d, k] = jnp.where(upper, half(second, 1), half(first, 0))


def pack_kernel(ends, picked, out):
    for h in range(2):
        for q in range(8):
            out[h, q, :, 0:16] = ends[h, q]
            out[h, q, :, 16:24] = picked[q, h]


def advance_kernel(received, states, gain, new_states, fetched):
    factor = gain[...]
    carried = states[0]
    for s in range(received.shape[0]):
        fine = received[s, :, 0:16]
        change = fine - factor * states[s]
        carried = factor * carried + change
        new_states[s] = carried
        tile = received[s, :, 16:24]
        fetched[s, 0] = tile[:, 0:4]
        fetched[s, 1] = tile[:, 4:8]


def exchange(value, axes):
    return lax.all_to_all(value, axes, 0, 0, tiled=True)


def call(kernel, name, shapes, kinds, scratch=(), **more):
    outs = [jax.ShapeDtypeStruct(shape, jnp.float32) for shape in shapes]
    return pl.pallas_call(
        kernel,
        out_shape=outs,
        in_specs=kinds,
        out_specs=[VMEM] * len(outs),
        scratch_shapes=[pltpu.VMEM(shape, jnp.float32) for shape in scratch],
        compiler_params=PARAMS,
        name=name,
        **more,
    )


def body(states, diffusivity, coarse_gain, read_block, read_count):
    slices, thick, own_rows, lanes = states.shape
    y, zh = lax.axis_index("y"), lax.axis_index("zh")
    x, c = lax.axis_index("x"), lax.axis_index("c")
    ny, nx = lax.axis_size("y"), lax.axis_size("x")
    me = lax.axis_index(RING)
    cut = lax.axis_index(CUTS)
    tile_rows = 2 * own_rows
    wide = tile_rows + 2 * FINE
    half = slices // 2
    x_up = [(i, i + 1) for i in range(nx - 1)]
    x_down = [(i + 1, i) for i in range(nx - 1)]

    edge_rows = lax.dynamic_slice_in_dim(states, zh * (own_rows - FINE), FINE, 2)
    pairs = [(i, i + 2) for i in range(1, 2 * ny - 2, 2)]
    pairs += [(i, i - 2) for i in range(2, 2 * ny, 2)]
    side_rows = lax.ppermute(edge_rows, CUTS, pairs)

    padded = jnp.pad(diffusivity, ((0, 0), (FINE, FINE), (0, 0)))
    kappa = lax.dynamic_slice_in_dim(padded, y * tile_rows, wide, 1)
    around = lax.axis_size(CHIPS)
    ring = [
        lax.ppermute(kappa, CHIPS, [(i, (i - offset) % around) for i in range(around)])
        for offset in RING_OFFSETS[1:]
    ]

    block = jnp.concatenate([states, side_rows], axis=2)
    block, kappa, *ring = lax.optimization_barrier((block, kappa, *ring))
    own = exchange(block, RING).reshape(2, half, thick, own_rows + FINE, lanes)

    mine = jnp.stack([kappa, *ring])
    other = lax.ppermute(mine, "c", [(0, 1), (1, 0)])
    place = jnp.stack([c, lax.axis_index("zl")])
    part = (FINE, wide, lanes)
    k_first, k_second = call(
        gather_kernel, "gather", [part] * 2, [SMEM, VMEM, VMEM], [(2 * FINE, *part[1:])]
    )(place, mine, other)
    k_low = lax.ppermute(k_second, "x", x_up)
    k_high = lax.ppermute(k_first, "x", x_down)

    low = lax.ppermute(own[:, half // 2 :], "x", x_up)
    high = lax.ppermute(own[:, : half // 2], "x", x_down)

    flags = [y > 0, y < ny - 1, x > 0, x < nx - 1]
    edge = jnp.stack([flag.astype(jnp.int32) for flag in flags])
    deep = half * thick
    region = (deep + 2 * FINE, wide, lanes)
    coefficients = call(
        coefficient_kernel, "coefficients", [region] * 7, [SMEM] + [VMEM] * 4
    )(edge, k_low, k_first, k_second, k_high)
    fine, ends = call(
        fine_kernel,
        "fine",
        [(ny, deep // ny, tile_rows, lanes), (2, half, thick, own_rows, lanes)],
        [VMEM] * 10,
        [region],
    )(low, own, high, *coefficients)

    tiles = exchange(fine, "y")
    (picked,) = call(
        pick_kernel,
        "pick",
        [(slices, thick, 2 * BY, lanes)],
        [SMEM, SMEM, SMEM, VMEM],
    )(read_block.reshape(-1), read_count.reshape(-1), me[None], tiles)
    picked = exchange(picked, "y").reshape(ny, 2, thick, 2 * BY, lanes)
    (payload,) = call(
        pack_kernel, "pack", [(2, half, thick, own_rows + 2 * BY, lanes)], [VMEM] * 2
    )(ends, picked)
    received = exchange(
        payload.reshape(slices, thick, own_rows + 2 * BY, lanes), RING
    )
    gain = lax.dynamic_slice_in_dim(coarse_gain, cut * own_rows, own_rows, 1)
    new_states, fetched = call(
        advance_kernel,
        "advance",
        [states.shape, (slices, 2, thick, BY, lanes)],
        [VMEM] * 3,
    )(received, states, gain)
    return new_states, fetched[None]


def solution(mesh):
    grid = Mesh(mesh.devices.reshape(8, 2, 4, 4, 2), ("y", "zh", "x", "zl", "c"))
    placed = (P(None, SLAB, CUTS, None), P(SLAB, None, None), P(SLAB, None, None), P(), P())
    return jax.shard_map(
        body,
        mesh=grid,
        in_specs=placed,
        out_specs=(P(None, SLAB, CUTS, None), P(CUTS, None, None, SLAB, None, None)),
        check_vma=False,
    )
```

```python
import jax
import jax.numpy as jnp
from jax import lax
from jax.experimental import pallas as pl
from jax.experimental.pallas import tpu as pltpu
from jax.sharding import Mesh
from jax.sharding import PartitionSpec as P

FINE = 8
BY = 4
COURANT = 0.45

NEAR = ("zl", "c")
SLAB = ("x", "zl", "c")
CUTS = ("y", "zh")

VMEM = pl.BlockSpec(memory_space=pltpu.VMEM)
SMEM = pl.BlockSpec(memory_space=pltpu.SMEM)
PARAMS = pltpu.CompilerParams(vmem_limit_bytes=40 * 2**20)


def rows_kernel(place, kappa, *outs):
    thick, grid_rows, lanes = kappa.shape
    rows = outs[0].shape[1]
    for m, out in enumerate(outs):
        first = (place[0] ^ m) * (rows - 2 * FINE) - FINE
        for r in range(0, rows, 8):
            row = first + r
            fits = jnp.where(row >= 0, jnp.where(row < grid_rows, 1, 0), 0)
            start = pl.multiple_of(jnp.clip(row, 0, grid_rows - 8), 8)
            keep = jnp.full((8, lanes), fits) == 1
            for k in range(thick):
                tile = kappa[k, pl.ds(start, 8), :]
                out[k, r : r + 8] = jnp.where(keep, tile, 0.0)


def gather_kernel(place, *refs):
    *pieces, first, second, kappa = refs
    for m, piece in enumerate(pieces):
        j = place[0] ^ m
        for k in range(2):
            kappa[2 * j + k] = piece[k]
    for z in range(FINE):
        first[z] = kappa[z]
        second[z] = kappa[FINE + z]


def spread_kernel(slab, out):
    tiles, cuts = out.shape[0], slab.shape[0]
    nothing = jnp.zeros(out.shape[1:2] + (8,) + out.shape[3:], jnp.float32)
    for t in range(tiles):
        out[t, :, 0:8] = slab[2 * t - 1, :, 8:16] if t > 0 else nothing
        out[t, :, 8:24] = slab[2 * t]
        out[t, :, 24:40] = slab[2 * t + 1]
        out[t, :, 40:48] = slab[2 * t + 2, :, 0:8] if 2 * t + 2 < cuts else nothing


def coefficient_kernel(
    edge, low, first, second, high, c0, zp, zm, yp, ym, xp, xm
):
    depth, rows, lanes = c0.shape
    parts = (low, first, second, high)
    at = lambda z: parts[z // 8][z % 8]
    row = lax.broadcasted_iota(jnp.int32, (rows, lanes), 0)
    lane = lax.broadcasted_iota(jnp.int32, (rows, lanes), 1)
    inside = jnp.where(
        row < 8, edge[0], jnp.where(row >= rows - 8, edge[1], 1)
    ).astype(jnp.float32)
    below = inside * edge[2].astype(jnp.float32)
    above = inside * edge[3].astype(jnp.float32)
    not_first = jnp.where(lane == 0, 0.0, 1.0)
    not_last = jnp.where(lane == lanes - 1, 0.0, 1.0)
    down, here = 0.5 * (at(0) + at(1)), at(1)
    for z in range(1, depth - 1):
        mask = below if z < 8 else above if z >= depth - 8 else inside
        after = at(z + 1)
        up = 0.5 * (here + after)
        north = 0.5 * (here + pltpu.roll(here, rows - 1, 0))
        south = 0.5 * (here + pltpu.roll(here, 1, 0))
        east = 0.5 * (here + pltpu.roll(here, lanes - 1, 1) * not_last)
        west = 0.5 * (here + pltpu.roll(here, 1, 1) * not_first)
        total = ((up + down) + (north + south)) + (east + west)
        c0[z] = ((1.0 - COURANT) - total) * mask
        zp[z] = up * mask
        zm[z] = (down + COURANT) * mask
        yp[z] = north * mask
        ym[z] = south * mask
        xp[z] = east * (mask * not_last)
        xm[z] = west * (mask * not_first)
        down, here = up, after


def fine_kernel(low, own, high, c0, zp, zm, yp, ym, xp, xm, out, u):
    depth, rows, lanes = u.shape

    def given(z):
        part, layer = (low, z) if z < 8 else (own, z - 8) if z < 24 else (high, z - 24)
        return part[layer // 2, layer % 2]

    for step in range(1, FINE + 1):
        at = given if step == 1 else (lambda z: u[z])
        below, here = at(step - 1), at(step)
        for z in range(step, depth - step):
            above = at(z + 1)
            new = (
                (c0[z] * here + zp[z] * above)
                + (zm[z] * below + yp[z] * pltpu.roll(here, rows - 1, 0))
                + (
                    ym[z] * pltpu.roll(here, 1, 0)
                    + xp[z] * pltpu.roll(here, lanes - 1, 1)
                )
                + xm[z] * pltpu.roll(here, 1, 1)
            )
            if step < FINE:
                u[z] = new
            else:
                out[(z - 8) // 2, z % 2] = new[8 : rows - 8]
            below, here = here, above


def pick_kernel(blocks, counts, me, tiles, out):
    slices, _, _, lanes = out.shape
    upper = lax.broadcasted_iota(jnp.int32, (2 * BY, lanes), 0) >= BY
    for d in range(slices):
        count = counts[d * slices + me[0]]
        first = blocks[(d * slices + me[0]) * 2]
        second = blocks[(d * slices + me[0]) * 2 + 1]
        for k in range(2):
            def half(block, slot):
                start = pl.multiple_of(((block >> 1) & 3) * 8, 8)
                tile = tiles[(block >> 3) & 7, k, pl.ds(start, 8), :]
                turned = pltpu.roll(tile, BY, 0)
                fits = jnp.where((block & 1) == slot, 1, 0)
                live = jnp.where(slot < count, 1, 0)
                chosen = jnp.where(jnp.full(tile.shape, fits) == 1, tile, turned)
                return jnp.where(jnp.full(tile.shape, live) == 1, chosen, 0.0)

            out[d, k, 0:16] = tiles[d // 2, k, 16 * (d % 2) : 16 * (d % 2) + 16]
            out[d, k, 16:24] = jnp.where(upper, half(second, 1), half(first, 0))


def advance_kernel(received, states, gain, new_states, fetched):
    factor = gain[...]
    carried = states[0]
    for s in range(received.shape[0]):
        fine = received[s, :, 0:16]
        change = fine - factor * states[s]
        carried = factor * carried + change
        new_states[s] = carried
        tile = received[s, :, 16:24]
        fetched[s, 0] = tile[:, 0:4]
        fetched[s, 1] = tile[:, 4:8]


def exchange(value, axes):
    return lax.all_to_all(value, axes, 0, 0, tiled=True)


def call(kernel, name, shapes, kinds, scratch=(), **more):
    outs = [jax.ShapeDtypeStruct(shape, jnp.float32) for shape in shapes]
    return pl.pallas_call(
        kernel,
        out_shape=outs,
        in_specs=kinds,
        out_specs=[VMEM] * len(outs),
        scratch_shapes=[pltpu.VMEM(shape, jnp.float32) for shape in scratch],
        compiler_params=PARAMS,
        name=name,
        **more,
    )


def body(states, diffusivity, coarse_gain, read_block, read_count):
    slices, thick, own_rows, lanes = states.shape
    x, near, cut = lax.axis_index("x"), lax.axis_index(NEAR), lax.axis_index(CUTS)
    nx, tiles = lax.axis_size("x"), lax.axis_size(NEAR)
    tile_rows = diffusivity.shape[1] // tiles
    wide = tile_rows + 2 * FINE
    deep = tiles * thick
    x_up = [(i, i + 1) for i in range(nx - 1)]
    x_down = [(i + 1, i) for i in range(nx - 1)]

    place = near[None]
    sends = call(rows_kernel, "rows", [(thick, wide, lanes)] * tiles, [SMEM, VMEM])(
        place, diffusivity
    )
    pieces = [
        lax.ppermute(send, NEAR, [(i, i ^ m) for i in range(tiles)]) if m else send
        for m, send in enumerate(sends)
    ]

    slab = exchange(states, CUTS)
    early = 7
    slab, *pieces[:early] = lax.optimization_barrier((slab, *pieces[:early]))
    (spread,) = call(
        spread_kernel, "spread", [(tiles, thick, wide, lanes)], [VMEM]
    )(slab)
    own = exchange(spread, NEAR)
    low = lax.ppermute(own[tiles // 2 :], "x", x_up)
    high = lax.ppermute(own[: tiles // 2], "x", x_down)

    part = (FINE, wide, lanes)
    k_first, k_second = call(
        gather_kernel,
        "gather",
        [part] * 2,
        [SMEM] + [VMEM] * tiles,
        [(deep, wide, lanes)],
    )(place, *pieces)
    k_low = lax.ppermute(k_second, "x", x_up)
    k_high = lax.ppermute(k_first, "x", x_down)

    flags = [near > 0, near < tiles - 1, x > 0, x < nx - 1]
    edge = jnp.stack([flag.astype(jnp.int32) for flag in flags])
    region = (deep + 2 * FINE, wide, lanes)
    coefficients = call(
        coefficient_kernel, "coefficients", [region] * 7, [SMEM] + [VMEM] * 4
    )(edge, k_low, k_first, k_second, k_high)
    (fine,) = call(
        fine_kernel,
        "fine",
        [(tiles, thick, tile_rows, lanes)],
        [VMEM] * 10,
        [region],
    )(low, own, high, *coefficients)

    rows = exchange(fine, NEAR)
    (payload,) = call(
        pick_kernel,
        "pick",
        [(slices, thick, own_rows + 2 * BY, lanes)],
        [SMEM, SMEM, SMEM, VMEM],
    )(read_block.reshape(-1), read_count.reshape(-1), cut[None], rows)
    received = exchange(payload, CUTS)
    gain = lax.dynamic_slice_in_dim(coarse_gain, cut * own_rows, own_rows, 1)
    new_states, fetched = call(
        advance_kernel,
        "advance",
        [states.shape, (slices, 2, thick, BY, lanes)],
        [VMEM] * 3,
    )(received, states, gain)
    return new_states, fetched[None]


def solution(mesh):
    grid = Mesh(mesh.devices.reshape(8, 2, 4, 4, 2), ("y", "zh", "x", "zl", "c"))
    placed = (P(None, SLAB, CUTS, None), P(SLAB, None, None), P(SLAB, None, None), P(), P())
    return jax.shard_map(
        body,
        mesh=grid,
        in_specs=placed,
        out_specs=(P(None, SLAB, CUTS, None), P(CUTS, None, None, SLAB, None, None)),
        check_vma=False,
    )
```

```python
import jax
import jax.numpy as jnp
from jax import lax
from jax.experimental import pallas as pl
from jax.experimental.pallas import tpu as pltpu
from jax.sharding import Mesh
from jax.sharding import PartitionSpec as P

FINE = 8
BY = 4
COURANT = 0.45

RING = ("zh", "zl", "c")
SLAB = ("x", "zl", "c")
CUTS = ("y", "zh")
NEAR = ("zl", "c")

VMEM = pl.BlockSpec(memory_space=pltpu.VMEM)
SMEM = pl.BlockSpec(memory_space=pltpu.SMEM)
PARAMS = pltpu.CompilerParams(vmem_limit_bytes=40 * 2**20)


def join_kernel(own, south, north, first, second):
    for out, start in ((first, 0), (second, 4)):
        for j in range(4):
            for k in range(2):
                layer = 2 * j + k
                out[layer, 0:8] = south[start + j, k]
                out[layer, 8:24] = own[0, start + j, k]
                out[layer, 24:40] = own[1, start + j, k]
                out[layer, 40:48] = north[start + j, k]


def coefficient_kernel(
    edge, low, own, high, c0, zp, zm, yp, ym, xp, xm
):
    depth, rows, lanes = c0.shape

    def at(z):
        return low[z] if z < 8 else own[z - 8] if z < 24 else high[z - 24]

    row = lax.broadcasted_iota(jnp.int32, (rows, lanes), 0)
    lane = lax.broadcasted_iota(jnp.int32, (rows, lanes), 1)
    inside = jnp.where(
        row < 8, edge[0], jnp.where(row >= rows - 8, edge[1], 1)
    ).astype(jnp.float32)
    below = inside * edge[2].astype(jnp.float32)
    above = inside * edge[3].astype(jnp.float32)
    not_first = jnp.where(lane == 0, 0.0, 1.0)
    not_last = jnp.where(lane == lanes - 1, 0.0, 1.0)
    down, here = 0.5 * (at(0) + at(1)), at(1)
    for z in range(1, depth - 1):
        mask = below if z < 8 else above if z >= depth - 8 else inside
        after = at(z + 1)
        up = 0.5 * (here + after)
        north = 0.5 * (here + pltpu.roll(here, rows - 1, 0))
        south = 0.5 * (here + pltpu.roll(here, 1, 0))
        east = 0.5 * (here + pltpu.roll(here, lanes - 1, 1) * not_last)
        west = 0.5 * (here + pltpu.roll(here, 1, 1) * not_first)
        total = ((up + down) + (north + south)) + (east + west)
        c0[z] = ((1.0 - COURANT) - total) * mask
        zp[z] = up * mask
        zm[z] = (down + COURANT) * mask
        yp[z] = north * mask
        ym[z] = south * mask
        xp[z] = east * (mask * not_last)
        xm[z] = west * (mask * not_first)
        down, here = up, after


def fine_kernel(low, first, second, high, c0, zp, zm, yp, ym, xp, xm, out, ends, u):
    depth, rows, lanes = u.shape
    parts = (low, first, second, high)

    def given(z):
        return parts[z // 8][z % 8]

    for step in range(1, FINE + 1):
        at = given if step == 1 else (lambda z: u[z])
        below, here = at(step - 1), at(step)
        for z in range(step, depth - step):
            above = at(z + 1)
            new = (
                (c0[z] * here + zp[z] * above)
                + (zm[z] * below + yp[z] * pltpu.roll(here, rows - 1, 0))
                + (
                    ym[z] * pltpu.roll(here, 1, 0)
                    + xp[z] * pltpu.roll(here, lanes - 1, 1)
                )
                + xm[z] * pltpu.roll(here, 1, 1)
            )
            if step < FINE:
                u[z] = new
            else:
                q, k = (z - 8) // 2, z % 2
                out[q, k] = new[8 : rows - 8]
                ends[0, q, k] = new[8:24]
                ends[1, q, k] = new[24:40]
            below, here = here, above


def pick_kernel(blocks, counts, me, tiles, out):
    slices = out.shape[0]
    upper = lax.broadcasted_iota(jnp.int32, out.shape[2:], 0) >= BY
    for d in range(slices):
        count = counts[d * slices + me[0]]
        first = blocks[(d * slices + me[0]) * 2]
        second = blocks[(d * slices + me[0]) * 2 + 1]
        for k in range(2):
            def half(block, slot):
                start = pl.multiple_of(((block >> 1) & 3) * 8, 8)
                tile = tiles[(block >> 3) & 7, k, pl.ds(start, 8), :]
                turned = pltpu.roll(tile, BY, 0)
                fits = jnp.where((block & 1) == slot, 1, 0)
                live = jnp.where(slot < count, 1, 0)
                chosen = jnp.where(jnp.full(tile.shape, fits) == 1, tile, turned)
                return jnp.where(jnp.full(tile.shape, live) == 1, chosen, 0.0)

            out[d, k] = jnp.where(upper, half(second, 1), half(first, 0))


def pack_kernel(ends, picked, out):
    for h in range(2):
        for q in range(8):
            out[h, q, :, 0:16] = ends[h, q]
            out[h, q, :, 16:24] = picked[q, h]


def advance_kernel(received, states, gain, new_states, fetched):
    factor = gain[...]
    carried = states[0]
    for s in range(received.shape[0]):
        fine = received[s, :, 0:16]
        change = fine - factor * states[s]
        carried = factor * carried + change
        new_states[s] = carried
        tile = received[s, :, 16:24]
        fetched[s, 0] = tile[:, 0:4]
        fetched[s, 1] = tile[:, 4:8]


def exchange(value, axes):
    return lax.all_to_all(value, axes, 0, 0, tiled=True)


def call(kernel, name, shapes, kinds, scratch=(), **more):
    outs = [jax.ShapeDtypeStruct(shape, jnp.float32) for shape in shapes]
    return pl.pallas_call(
        kernel,
        out_shape=outs,
        in_specs=kinds,
        out_specs=[VMEM] * len(outs),
        scratch_shapes=[pltpu.VMEM(shape, jnp.float32) for shape in scratch],
        compiler_params=PARAMS,
        name=name,
        **more,
    )


def body(states, diffusivity, coarse_gain, read_block, read_count):
    slices, thick, own_rows, lanes = states.shape
    y = lax.axis_index("y")
    x = lax.axis_index("x")
    ny, nx = lax.axis_size("y"), lax.axis_size("x")
    me = lax.axis_index(RING)
    cut = lax.axis_index(CUTS)
    tile_rows = 2 * own_rows
    wide = tile_rows + 2 * FINE
    half = slices // 2
    x_up = [(i, i + 1) for i in range(nx - 1)]
    x_down = [(i + 1, i) for i in range(nx - 1)]

    y_up = [(i, i + 1) for i in range(ny - 1)]
    y_down = [(i + 1, i) for i in range(ny - 1)]

    padded = jnp.pad(diffusivity, ((0, 0), (FINE, FINE), (0, 0)))
    kappa = lax.dynamic_slice_in_dim(padded, y * tile_rows, wide, 1)
    kappas = lax.all_gather(kappa, NEAR, tiled=True)

    own = exchange(states, RING).reshape(2, half, thick, own_rows, lanes)
    own, kappas = lax.optimization_barrier((own, kappas))
    south = lax.ppermute(own[1, :, :, own_rows - FINE :], "y", y_up)
    north = lax.ppermute(own[0, :, :, :FINE], "y", y_down)
    k_low = lax.ppermute(kappas[half:], "x", x_up)
    k_high = lax.ppermute(kappas[:half], "x", x_down)
    part = (FINE, wide, lanes)
    first, second = call(join_kernel, "join", [part] * 2, [VMEM] * 3)(own, south, north)
    low = lax.ppermute(second, "x", x_up)
    high = lax.ppermute(first, "x", x_down)

    flags = [y > 0, y < ny - 1, x > 0, x < nx - 1]
    edge = jnp.stack([flag.astype(jnp.int32) for flag in flags])
    deep = half * thick
    region = (deep + 2 * FINE, wide, lanes)
    coefficients = call(
        coefficient_kernel, "coefficients", [region] * 7, [SMEM] + [VMEM] * 3
    )(edge, k_low, kappas, k_high)
    fine, ends = call(
        fine_kernel,
        "fine",
        [(ny, deep // ny, tile_rows, lanes), (2, half, thick, own_rows, lanes)],
        [VMEM] * 11,
        [region],
    )(low, first, second, high, *coefficients)

    tiles = exchange(fine, "y")
    (picked,) = call(
        pick_kernel,
        "pick",
        [(slices, thick, 2 * BY, lanes)],
        [SMEM, SMEM, SMEM, VMEM],
    )(read_block.reshape(-1), read_count.reshape(-1), me[None], tiles)
    picked = exchange(picked, "y").reshape(ny, 2, thick, 2 * BY, lanes)
    (payload,) = call(
        pack_kernel, "pack", [(2, half, thick, own_rows + 2 * BY, lanes)], [VMEM] * 2
    )(ends, picked)
    received = exchange(
        payload.reshape(slices, thick, own_rows + 2 * BY, lanes), RING
    )
    gain = lax.dynamic_slice_in_dim(coarse_gain, cut * own_rows, own_rows, 1)
    new_states, fetched = call(
        advance_kernel,
        "advance",
        [states.shape, (slices, 2, thick, BY, lanes)],
        [VMEM] * 3,
    )(received, states, gain)
    return new_states, fetched[None]


def solution(mesh):
    grid = Mesh(mesh.devices.reshape(8, 2, 4, 4, 2), ("y", "zh", "x", "zl", "c"))
    placed = (P(None, SLAB, CUTS, None), P(SLAB, None, None), P(SLAB, None, None), P(), P())
    return jax.shard_map(
        body,
        mesh=grid,
        in_specs=placed,
        out_specs=(P(None, SLAB, CUTS, None), P(CUTS, None, None, SLAB, None, None)),
        check_vma=False,
    )
```

```python
import jax
import jax.numpy as jnp
from jax import lax
from jax.experimental import pallas as pl
from jax.experimental.pallas import tpu as pltpu
from jax.sharding import Mesh
from jax.sharding import PartitionSpec as P

FINE = 8
BY = 4
COURANT = 0.45

RING = ("zh", "zl", "c")
SLAB = ("x", "zl", "c")
CUTS = ("y", "zh")
NEAR = ("zl", "c")

VMEM = pl.BlockSpec(memory_space=pltpu.VMEM)
SMEM = pl.BlockSpec(memory_space=pltpu.SMEM)
PARAMS = pltpu.CompilerParams(vmem_limit_bytes=40 * 2**20)


def join_kernel(own, south, north, first, second):
    for out, start in ((first, 0), (second, 4)):
        for j in range(4):
            for k in range(2):
                layer = 2 * j + k
                out[layer, 0:8] = south[start + j, k]
                out[layer, 8:24] = own[0, start + j, k]
                out[layer, 24:40] = own[1, start + j, k]
                out[layer, 40:48] = north[start + j, k]


def coefficient_kernel(
    edge, low, own, high, c0, zp, zm, yp, ym, xp, xm
):
    depth, rows, lanes = c0.shape

    def at(z):
        return low[z] if z < 8 else own[z - 8] if z < 24 else high[z - 24]

    row = lax.broadcasted_iota(jnp.int32, (rows, lanes), 0)
    lane = lax.broadcasted_iota(jnp.int32, (rows, lanes), 1)
    inside = jnp.where(
        row < 8, edge[0], jnp.where(row >= rows - 8, edge[1], 1)
    ).astype(jnp.float32)
    below = inside * edge[2].astype(jnp.float32)
    above = inside * edge[3].astype(jnp.float32)
    not_first = jnp.where(lane == 0, 0.0, 1.0)
    not_last = jnp.where(lane == lanes - 1, 0.0, 1.0)
    down, here = 0.5 * (at(0) + at(1)), at(1)
    for z in range(1, depth - 1):
        mask = below if z < 8 else above if z >= depth - 8 else inside
        after = at(z + 1)
        up = 0.5 * (here + after)
        north = 0.5 * (here + pltpu.roll(here, rows - 1, 0))
        south = 0.5 * (here + pltpu.roll(here, 1, 0))
        east = 0.5 * (here + pltpu.roll(here, lanes - 1, 1) * not_last)
        west = 0.5 * (here + pltpu.roll(here, 1, 1) * not_first)
        total = ((up + down) + (north + south)) + (east + west)
        c0[z] = ((1.0 - COURANT) - total) * mask
        zp[z] = up * mask
        zm[z] = (down + COURANT) * mask
        yp[z] = north * mask
        ym[z] = south * mask
        xp[z] = east * (mask * not_last)
        xm[z] = west * (mask * not_first)
        down, here = up, after


def advance_layer(coefficients, z, below, here, above):
    c0, zp, zm, yp, ym, xp, xm = coefficients
    rows, lanes = here.shape
    return (
        (c0[z] * here + zp[z] * above)
        + (zm[z] * below + yp[z] * pltpu.roll(here, rows - 1, 0))
        + (ym[z] * pltpu.roll(here, 1, 0) + xp[z] * pltpu.roll(here, lanes - 1, 1))
        + xm[z] * pltpu.roll(here, 1, 1)
    )


def inner_kernel(first, second, *refs):
    *coefficients, kept, u = refs
    for step in range(1, FINE):

        def at(z):
            if step == 1:
                return first[z - 8] if z < 16 else second[z - 16]
            return u[z - 8]

        lowest, end = 8 + step, 24 - step
        below, here = at(lowest - 1), at(lowest)
        for z in range(lowest, end):
            above = at(z + 1)
            new = advance_layer(coefficients, z, below, here, above)
            u[z - 8] = new
            if z < lowest + 2:
                kept[step - 1, z - lowest] = new
            if z >= end - 2:
                kept[step - 1, 4 + z - end] = new
            below, here = here, above


def fine_kernel(low, first, second, high, kept, *refs):
    *coefficients, out, ends, u = refs
    rows = low.shape[1]
    parts = (low, first, second, high)
    for step in range(1, FINE + 1):
        done = step - 1

        def at(z):
            if done == 0:
                return parts[z // 8][z % 8]
            if z < 8 + done or z >= 24 - done:
                return u[z]
            return kept[done - 1, z - 8 - done if z < 16 else 4 + z - 24 + done]

        for start in (step, 24 - step):
            below, here = at(start - 1), at(start)
            for z in range(start, start + 8):
                above = at(z + 1)
                new = advance_layer(coefficients, z, below, here, above)
                if step < FINE:
                    u[z] = new
                else:
                    q, k = (z - 8) // 2, z % 2
                    out[q, k] = new[8 : rows - 8]
                    ends[0, q, k] = new[8:24]
                    ends[1, q, k] = new[24:40]
                below, here = here, above


def pick_kernel(blocks, counts, me, tiles, out):
    slices = out.shape[0]
    upper = lax.broadcasted_iota(jnp.int32, out.shape[2:], 0) >= BY
    for d in range(slices):
        count = counts[d * slices + me[0]]
        first = blocks[(d * slices + me[0]) * 2]
        second = blocks[(d * slices + me[0]) * 2 + 1]
        for k in range(2):
            def half(block, slot):
                start = pl.multiple_of(((block >> 1) & 3) * 8, 8)
                tile = tiles[(block >> 3) & 7, k, pl.ds(start, 8), :]
                turned = pltpu.roll(tile, BY, 0)
                fits = jnp.where((block & 1) == slot, 1, 0)
                live = jnp.where(slot < count, 1, 0)
                chosen = jnp.where(jnp.full(tile.shape, fits) == 1, tile, turned)
                return jnp.where(jnp.full(tile.shape, live) == 1, chosen, 0.0)

            out[d, k] = jnp.where(upper, half(second, 1), half(first, 0))


def pack_kernel(ends, picked, out):
    for h in range(2):
        for q in range(8):
            out[h, q, :, 0:16] = ends[h, q]
            out[h, q, :, 16:24] = picked[q, h]


def advance_kernel(received, states, gain, new_states, fetched):
    factor = gain[...]
    carried = states[0]
    for s in range(received.shape[0]):
        fine = received[s, :, 0:16]
        change = fine - factor * states[s]
        carried = factor * carried + change
        new_states[s] = carried
        tile = received[s, :, 16:24]
        fetched[s, 0] = tile[:, 0:4]
        fetched[s, 1] = tile[:, 4:8]


def exchange(value, axes):
    return lax.all_to_all(value, axes, 0, 0, tiled=True)


def call(kernel, name, shapes, kinds, scratch=(), **more):
    outs = [jax.ShapeDtypeStruct(shape, jnp.float32) for shape in shapes]
    return pl.pallas_call(
        kernel,
        out_shape=outs,
        in_specs=kinds,
        out_specs=[VMEM] * len(outs),
        scratch_shapes=[pltpu.VMEM(shape, jnp.float32) for shape in scratch],
        compiler_params=PARAMS,
        name=name,
        **more,
    )


def body(states, diffusivity, coarse_gain, read_block, read_count):
    slices, thick, own_rows, lanes = states.shape
    y = lax.axis_index("y")
    x = lax.axis_index("x")
    ny, nx = lax.axis_size("y"), lax.axis_size("x")
    me = lax.axis_index(RING)
    cut = lax.axis_index(CUTS)
    tile_rows = 2 * own_rows
    wide = tile_rows + 2 * FINE
    half = slices // 2
    x_up = [(i, i + 1) for i in range(nx - 1)]
    x_down = [(i + 1, i) for i in range(nx - 1)]

    y_up = [(i, i + 1) for i in range(ny - 1)]
    y_down = [(i + 1, i) for i in range(ny - 1)]

    padded = jnp.pad(diffusivity, ((0, 0), (FINE, FINE), (0, 0)))
    kappa = lax.dynamic_slice_in_dim(padded, y * tile_rows, wide, 1)
    kappas = lax.all_gather(kappa, NEAR, tiled=True)

    own = exchange(states, RING).reshape(2, half, thick, own_rows, lanes)
    own, kappas = lax.optimization_barrier((own, kappas))
    south = lax.ppermute(own[1, :, :, own_rows - FINE :], "y", y_up)
    north = lax.ppermute(own[0, :, :, :FINE], "y", y_down)
    k_low = lax.ppermute(kappas[half:], "x", x_up)
    k_high = lax.ppermute(kappas[:half], "x", x_down)
    part = (FINE, wide, lanes)
    first, second = call(join_kernel, "join", [part] * 2, [VMEM] * 3)(own, south, north)
    low = lax.ppermute(second, "x", x_up)
    high = lax.ppermute(first, "x", x_down)

    flags = [y > 0, y < ny - 1, x > 0, x < nx - 1]
    edge = jnp.stack([flag.astype(jnp.int32) for flag in flags])
    deep = half * thick
    region = (deep + 2 * FINE, wide, lanes)
    coefficients = call(
        coefficient_kernel, "coefficients", [region] * 7, [SMEM] + [VMEM] * 3
    )(edge, k_low, kappas, k_high)
    (kept,) = call(
        inner_kernel, "inner", [(FINE - 1, 4, *part[1:])], [VMEM] * 9, [(deep, *part[1:])]
    )(first, second, *coefficients)
    fine, ends = call(
        fine_kernel,
        "fine",
        [(ny, deep // ny, tile_rows, lanes), (2, half, thick, own_rows, lanes)],
        [VMEM] * 12,
        [region],
    )(low, first, second, high, kept, *coefficients)

    tiles = exchange(fine, "y")
    (picked,) = call(
        pick_kernel,
        "pick",
        [(slices, thick, 2 * BY, lanes)],
        [SMEM, SMEM, SMEM, VMEM],
    )(read_block.reshape(-1), read_count.reshape(-1), me[None], tiles)
    picked = exchange(picked, "y").reshape(ny, 2, thick, 2 * BY, lanes)
    (payload,) = call(
        pack_kernel, "pack", [(2, half, thick, own_rows + 2 * BY, lanes)], [VMEM] * 2
    )(ends, picked)
    received = exchange(
        payload.reshape(slices, thick, own_rows + 2 * BY, lanes), RING
    )
    gain = lax.dynamic_slice_in_dim(coarse_gain, cut * own_rows, own_rows, 1)
    new_states, fetched = call(
        advance_kernel,
        "advance",
        [states.shape, (slices, 2, thick, BY, lanes)],
        [VMEM] * 3,
    )(received, states, gain)
    return new_states, fetched[None]


def solution(mesh):
    grid = Mesh(mesh.devices.reshape(8, 2, 4, 4, 2), ("y", "zh", "x", "zl", "c"))
    placed = (P(None, SLAB, CUTS, None), P(SLAB, None, None), P(SLAB, None, None), P(), P())
    return jax.shard_map(
        body,
        mesh=grid,
        in_specs=placed,
        out_specs=(P(None, SLAB, CUTS, None), P(CUTS, None, None, SLAB, None, None)),
        check_vma=False,
    )
```

```python
import jax
import jax.numpy as jnp
from jax import lax
from jax.experimental import pallas as pl
from jax.experimental.pallas import tpu as pltpu
from jax.sharding import Mesh
from jax.sharding import PartitionSpec as P

FINE = 8
BY = 4
COURANT = 0.45

RING = ("zh", "zl", "c")
SLAB = ("x", "zl", "c")
CUTS = ("y", "zh")

VMEM = pl.BlockSpec(memory_space=pltpu.VMEM)
SMEM = pl.BlockSpec(memory_space=pltpu.SMEM)
PARAMS = pltpu.CompilerParams(vmem_limit_bytes=40 * 2**20)


def load_kernel(states, kappa, out):
    for d in range(out.shape[0]):
        for k in range(2):
            out[d, 16 * k : 16 * k + 16] = states[d, k]
        out[d, 32:56] = kappa[d % 2]


def gather_kernel(place, mine, other, own, first, second, kappa):
    for part, source in ((place[0], mine), (1 - place[0], other)):
        for j in range(8):
            for h in range(2):
                kappa[2 * j + part, 24 * h : 24 * h + 24] = source[h, j]
    for z in range(FINE):
        own[z] = first[z] = kappa[z]
        own[FINE + z] = second[z] = kappa[FINE + z]


def join_kernel(own, south, north, first, second):
    for out, start in ((first, 0), (second, 4)):
        for j in range(4):
            for k in range(2):
                layer = 2 * j + k
                out[layer, 0:8] = south[start + j, k]
                out[layer, 8:24] = own[0, start + j, 16 * k : 16 * k + 16]
                out[layer, 24:40] = own[1, start + j, 16 * k : 16 * k + 16]
                out[layer, 40:48] = north[start + j, k]


def coefficient_kernel(
    edge, low, own, high, c0, zp, zm, yp, ym, xp, xm
):
    depth, rows, lanes = c0.shape

    def at(z):
        return low[z] if z < 8 else own[z - 8] if z < 24 else high[z - 24]

    row = lax.broadcasted_iota(jnp.int32, (rows, lanes), 0)
    lane = lax.broadcasted_iota(jnp.int32, (rows, lanes), 1)
    inside = jnp.where(
        row < 8, edge[0], jnp.where(row >= rows - 8, edge[1], 1)
    ).astype(jnp.float32)
    below = inside * edge[2].astype(jnp.float32)
    above = inside * edge[3].astype(jnp.float32)
    not_first = jnp.where(lane == 0, 0.0, 1.0)
    not_last = jnp.where(lane == lanes - 1, 0.0, 1.0)
    down, here = 0.5 * (at(0) + at(1)), at(1)
    for z in range(1, depth - 1):
        mask = below if z < 8 else above if z >= depth - 8 else inside
        after = at(z + 1)
        up = 0.5 * (here + after)
        north = 0.5 * (here + pltpu.roll(here, rows - 1, 0))
        south = 0.5 * (here + pltpu.roll(here, 1, 0))
        east = 0.5 * (here + pltpu.roll(here, lanes - 1, 1) * not_last)
        west = 0.5 * (here + pltpu.roll(here, 1, 1) * not_first)
        total = ((up + down) + (north + south)) + (east + west)
        c0[z] = ((1.0 - COURANT) - total) * mask
        zp[z] = up * mask
        zm[z] = (down + COURANT) * mask
        yp[z] = north * mask
        ym[z] = south * mask
        xp[z] = east * (mask * not_last)
        xm[z] = west * (mask * not_first)
        down, here = up, after


def advance_layer(coefficients, z, below, here, above):
    c0, zp, zm, yp, ym, xp, xm = coefficients
    rows, lanes = here.shape
    return (
        (c0[z] * here + zp[z] * above)
        + (zm[z] * below + yp[z] * pltpu.roll(here, rows - 1, 0))
        + (ym[z] * pltpu.roll(here, 1, 0) + xp[z] * pltpu.roll(here, lanes - 1, 1))
        + xm[z] * pltpu.roll(here, 1, 1)
    )


def inner_kernel(first, second, *refs):
    *coefficients, kept, u = refs
    for step in range(1, FINE):

        def at(z):
            if step == 1:
                return first[z - 8] if z < 16 else second[z - 16]
            return u[z - 8]

        lowest, end = 8 + step, 24 - step
        below, here = at(lowest - 1), at(lowest)
        for z in range(lowest, end):
            above = at(z + 1)
            new = advance_layer(coefficients, z, below, here, above)
            u[z - 8] = new
            if z < lowest + 2:
                kept[step - 1, z - lowest] = new
            if z >= end - 2:
                kept[step - 1, 4 + z - end] = new
            below, here = here, above


def fine_kernel(low, first, second, high, kept, *refs):
    *coefficients, out, ends, u = refs
    rows = low.shape[1]
    parts = (low, first, second, high)
    for step in range(1, FINE + 1):
        done = step - 1

        def at(z):
            if done == 0:
                return parts[z // 8][z % 8]
            if z < 8 + done or z >= 24 - done:
                return u[z]
            return kept[done - 1, z - 8 - done if z < 16 else 4 + z - 24 + done]

        for start in (step, 24 - step):
            below, here = at(start - 1), at(start)
            for z in range(start, start + 8):
                above = at(z + 1)
                new = advance_layer(coefficients, z, below, here, above)
                if step < FINE:
                    u[z] = new
                else:
                    q, k = (z - 8) // 2, z % 2
                    out[q, k] = new[8 : rows - 8]
                    ends[0, q, k] = new[8:24]
                    ends[1, q, k] = new[24:40]
                below, here = here, above


def pick_kernel(blocks, counts, me, tiles, out):
    slices = out.shape[0]
    upper = lax.broadcasted_iota(jnp.int32, out.shape[2:], 0) >= BY
    for d in range(slices):
        count = counts[d * slices + me[0]]
        first = blocks[(d * slices + me[0]) * 2]
        second = blocks[(d * slices + me[0]) * 2 + 1]
        for k in range(2):
            def half(block, slot):
                start = pl.multiple_of(((block >> 1) & 3) * 8, 8)
                tile = tiles[(block >> 3) & 7, k, pl.ds(start, 8), :]
                turned = pltpu.roll(tile, BY, 0)
                fits = jnp.where((block & 1) == slot, 1, 0)
                live = jnp.where(slot < count, 1, 0)
                chosen = jnp.where(jnp.full(tile.shape, fits) == 1, tile, turned)
                return jnp.where(jnp.full(tile.shape, live) == 1, chosen, 0.0)

            out[d, k] = jnp.where(upper, half(second, 1), half(first, 0))


def pack_kernel(ends, picked, out):
    for h in range(2):
        for q in range(8):
            out[h, q, :, 0:16] = ends[h, q]
            out[h, q, :, 16:24] = picked[q, h]


def advance_kernel(received, states, gain, new_states, fetched):
    factor = gain[...]
    carried = states[0]
    for s in range(received.shape[0]):
        fine = received[s, :, 0:16]
        change = fine - factor * states[s]
        carried = factor * carried + change
        new_states[s] = carried
        tile = received[s, :, 16:24]
        fetched[s, 0] = tile[:, 0:4]
        fetched[s, 1] = tile[:, 4:8]


def exchange(value, axes):
    return lax.all_to_all(value, axes, 0, 0, tiled=True)


def call(kernel, name, shapes, kinds, scratch=(), **more):
    outs = [jax.ShapeDtypeStruct(shape, jnp.float32) for shape in shapes]
    return pl.pallas_call(
        kernel,
        out_shape=outs,
        in_specs=kinds,
        out_specs=[VMEM] * len(outs),
        scratch_shapes=[pltpu.VMEM(shape, jnp.float32) for shape in scratch],
        compiler_params=PARAMS,
        name=name,
        **more,
    )


def body(states, diffusivity, coarse_gain, read_block, read_count):
    slices, thick, own_rows, lanes = states.shape
    y = lax.axis_index("y")
    x = lax.axis_index("x")
    ny, nx = lax.axis_size("y"), lax.axis_size("x")
    me = lax.axis_index(RING)
    cut = lax.axis_index(CUTS)
    tile_rows = 2 * own_rows
    wide = tile_rows + 2 * FINE
    half = slices // 2
    x_up = [(i, i + 1) for i in range(nx - 1)]
    x_down = [(i + 1, i) for i in range(nx - 1)]

    y_up = [(i, i + 1) for i in range(ny - 1)]
    y_down = [(i + 1, i) for i in range(ny - 1)]

    padded = jnp.pad(diffusivity, ((0, 0), (FINE, FINE), (0, 0)))
    window = y * tile_rows + lax.axis_index("zh") * (wide // 2)
    kappa = lax.dynamic_slice_in_dim(padded, window, wide // 2, 1)
    layers = thick * own_rows
    packed = layers + wide // 2
    (load,) = call(
        load_kernel, "load", [(slices, packed, lanes)], [VMEM] * 2
    )(states, kappa)
    own = exchange(load, RING).reshape(2, half, packed, lanes)
    ends_of = own[:, :, :layers].reshape(2, half, thick, own_rows, lanes)
    south = lax.ppermute(ends_of[1, :, :, own_rows - FINE :], "y", y_up)
    north = lax.ppermute(ends_of[0, :, :, :FINE], "y", y_down)
    part = (FINE, wide, lanes)
    mine = own[:, :, layers:]
    other = lax.ppermute(mine, "c", [(0, 1), (1, 0)])
    kappas, k_first, k_second = call(
        gather_kernel,
        "gather",
        [(2 * FINE, wide, lanes), part, part],
        [SMEM, VMEM, VMEM],
        [(2 * FINE, wide, lanes)],
    )(lax.axis_index("c")[None], mine, other)
    k_low = lax.ppermute(k_second, "x", x_up)
    k_high = lax.ppermute(k_first, "x", x_down)
    first, second = call(join_kernel, "join", [part] * 2, [VMEM] * 3)(own, south, north)
    low = lax.ppermute(second, "x", x_up)
    high = lax.ppermute(first, "x", x_down)

    flags = [y > 0, y < ny - 1, x > 0, x < nx - 1]
    edge = jnp.stack([flag.astype(jnp.int32) for flag in flags])
    deep = half * thick
    region = (deep + 2 * FINE, wide, lanes)
    coefficients = call(
        coefficient_kernel, "coefficients", [region] * 7, [SMEM] + [VMEM] * 3
    )(edge, k_low, kappas, k_high)
    (kept,) = call(
        inner_kernel, "inner", [(FINE - 1, 4, *part[1:])], [VMEM] * 9, [(deep, *part[1:])]
    )(first, second, *coefficients)
    fine, ends = call(
        fine_kernel,
        "fine",
        [(ny, deep // ny, tile_rows, lanes), (2, half, thick, own_rows, lanes)],
        [VMEM] * 12,
        [region],
    )(low, first, second, high, kept, *coefficients)

    tiles = exchange(fine, "y")
    (picked,) = call(
        pick_kernel,
        "pick",
        [(slices, thick, 2 * BY, lanes)],
        [SMEM, SMEM, SMEM, VMEM],
    )(read_block.reshape(-1), read_count.reshape(-1), me[None], tiles)
    picked = exchange(picked, "y").reshape(ny, 2, thick, 2 * BY, lanes)
    (payload,) = call(
        pack_kernel, "pack", [(2, half, thick, own_rows + 2 * BY, lanes)], [VMEM] * 2
    )(ends, picked)
    received = exchange(
        payload.reshape(slices, thick, own_rows + 2 * BY, lanes), RING
    )
    gain = lax.dynamic_slice_in_dim(coarse_gain, cut * own_rows, own_rows, 1)
    new_states, fetched = call(
        advance_kernel,
        "advance",
        [states.shape, (slices, 2, thick, BY, lanes)],
        [VMEM] * 3,
    )(received, states, gain)
    return new_states, fetched[None]


def solution(mesh):
    grid = Mesh(mesh.devices.reshape(8, 2, 4, 4, 2), ("y", "zh", "x", "zl", "c"))
    placed = (P(None, SLAB, CUTS, None), P(SLAB, None, None), P(SLAB, None, None), P(), P())
    return jax.shard_map(
        body,
        mesh=grid,
        in_specs=placed,
        out_specs=(P(None, SLAB, CUTS, None), P(CUTS, None, None, SLAB, None, None)),
        check_vma=False,
    )
```

```python
import jax
import jax.numpy as jnp
from jax import lax
from jax.experimental import pallas as pl
from jax.experimental.pallas import tpu as pltpu
from jax.sharding import Mesh
from jax.sharding import PartitionSpec as P

FINE = 8
BY = 4
COURANT = 0.45

RING = ("zh", "zl", "c")
SLAB = ("x", "zl", "c")
CUTS = ("y", "zh")

VMEM = pl.BlockSpec(memory_space=pltpu.VMEM)
SMEM = pl.BlockSpec(memory_space=pltpu.SMEM)
PARAMS = pltpu.CompilerParams(vmem_limit_bytes=40 * 2**20)


def load_kernel(skip, states, kappa, out):
    rows, lanes = kappa.shape[1:]
    for r in range(0, rows, 8):
        row = skip[0] + r
        fits = jnp.where(row >= 0, jnp.where(row < rows, 1, 0), 0)
        start = pl.multiple_of(jnp.clip(row, 0, rows - 8), 8)
        keep = jnp.full((8, lanes), fits) == 1
        for k in range(2):
            tile = jnp.where(keep, kappa[k, pl.ds(start, 8), :], 0.0)
            for d in range(k, out.shape[0], 2):
                out[d, 32 + r : 40 + r] = tile
    for d in range(out.shape[0]):
        for k in range(2):
            out[d, 16 * k : 16 * k + 16] = states[d, k]


def gather_kernel(place, mine, other, own, first, second, kappa):
    for part, source in ((place[0], mine), (1 - place[0], other)):
        for j in range(8):
            for h in range(2):
                kappa[2 * j + part, 24 * h : 24 * h + 24] = source[h, j]
    for z in range(FINE):
        own[z] = first[z] = kappa[z]
        own[FINE + z] = second[z] = kappa[FINE + z]


def join_kernel(own, south, north, first, second):
    for out, start in ((first, 0), (second, 4)):
        for j in range(4):
            for k in range(2):
                layer = 2 * j + k
                out[layer, 0:8] = south[start + j, k]
                out[layer, 8:24] = own[0, start + j, 16 * k : 16 * k + 16]
                out[layer, 24:40] = own[1, start + j, 16 * k : 16 * k + 16]
                out[layer, 40:48] = north[start + j, k]


def coefficient_kernel(
    edge, low, own, high, c0, zp, zm, yp, ym, xp, xm
):
    depth, rows, lanes = c0.shape

    def at(z):
        return low[z] if z < 8 else own[z - 8] if z < 24 else high[z - 24]

    row = lax.broadcasted_iota(jnp.int32, (rows, lanes), 0)
    lane = lax.broadcasted_iota(jnp.int32, (rows, lanes), 1)
    inside = jnp.where(
        row < 8, edge[0], jnp.where(row >= rows - 8, edge[1], 1)
    ).astype(jnp.float32)
    below = inside * edge[2].astype(jnp.float32)
    above = inside * edge[3].astype(jnp.float32)
    not_first = jnp.where(lane == 0, 0.0, 1.0)
    not_last = jnp.where(lane == lanes - 1, 0.0, 1.0)
    down, here = 0.5 * (at(0) + at(1)), at(1)
    for z in range(1, depth - 1):
        mask = below if z < 8 else above if z >= depth - 8 else inside
        after = at(z + 1)
        up = 0.5 * (here + after)
        north = 0.5 * (here + pltpu.roll(here, rows - 1, 0))
        south = 0.5 * (here + pltpu.roll(here, 1, 0))
        east = 0.5 * (here + pltpu.roll(here, lanes - 1, 1) * not_last)
        west = 0.5 * (here + pltpu.roll(here, 1, 1) * not_first)
        total = ((up + down) + (north + south)) + (east + west)
        c0[z] = ((1.0 - COURANT) - total) * mask
        zp[z] = up * mask
        zm[z] = (down + COURANT) * mask
        yp[z] = north * mask
        ym[z] = south * mask
        xp[z] = east * (mask * not_last)
        xm[z] = west * (mask * not_first)
        down, here = up, after


def advance_layer(coefficients, z, below, here, above):
    c0, zp, zm, yp, ym, xp, xm = coefficients
    rows, lanes = here.shape
    return (
        (c0[z] * here + zp[z] * above)
        + (zm[z] * below + yp[z] * pltpu.roll(here, rows - 1, 0))
        + (ym[z] * pltpu.roll(here, 1, 0) + xp[z] * pltpu.roll(here, lanes - 1, 1))
        + xm[z] * pltpu.roll(here, 1, 1)
    )


def inner_kernel(first, second, *refs):
    *coefficients, kept, u = refs
    for step in range(1, FINE):

        def at(z):
            if step == 1:
                return first[z - 8] if z < 16 else second[z - 16]
            return u[z - 8]

        lowest, end = 8 + step, 24 - step
        below, here = at(lowest - 1), at(lowest)
        for z in range(lowest, end):
            above = at(z + 1)
            new = advance_layer(coefficients, z, below, here, above)
            u[z - 8] = new
            if z < lowest + 2:
                kept[step - 1, z - lowest] = new
            if z >= end - 2:
                kept[step - 1, 4 + z - end] = new
            below, here = here, above


def fine_kernel(low, first, second, high, kept, *refs):
    *coefficients, out, ends, u = refs
    rows = low.shape[1]
    parts = (low, first, second, high)
    for step in range(1, FINE + 1):
        done = step - 1

        def at(z):
            if done == 0:
                return parts[z // 8][z % 8]
            if z < 8 + done or z >= 24 - done:
                return u[z]
            return kept[done - 1, z - 8 - done if z < 16 else 4 + z - 24 + done]

        for start in (step, 24 - step):
            below, here = at(start - 1), at(start)
            for z in range(start, start + 8):
                above = at(z + 1)
                new = advance_layer(coefficients, z, below, here, above)
                if step < FINE:
                    u[z] = new
                else:
                    q, k = (z - 8) // 2, z % 2
                    out[q, k] = new[8 : rows - 8]
                    ends[0, q, k] = new[8:24]
                    ends[1, q, k] = new[24:40]
                below, here = here, above


def pick_kernel(blocks, counts, me, tiles, out):
    slices = out.shape[0]
    upper = lax.broadcasted_iota(jnp.int32, out.shape[2:], 0) >= BY
    for d in range(slices):
        count = counts[d * slices + me[0]]
        first = blocks[(d * slices + me[0]) * 2]
        second = blocks[(d * slices + me[0]) * 2 + 1]
        for k in range(2):
            def half(block, slot):
                start = pl.multiple_of(((block >> 1) & 3) * 8, 8)
                tile = tiles[(block >> 3) & 7, k, pl.ds(start, 8), :]
                turned = pltpu.roll(tile, BY, 0)
                fits = jnp.where((block & 1) == slot, 1, 0)
                live = jnp.where(slot < count, 1, 0)
                chosen = jnp.where(jnp.full(tile.shape, fits) == 1, tile, turned)
                return jnp.where(jnp.full(tile.shape, live) == 1, chosen, 0.0)

            out[d, k] = jnp.where(upper, half(second, 1), half(first, 0))


def pack_kernel(ends, picked, out):
    for h in range(2):
        for q in range(8):
            out[h, q, :, 0:16] = ends[h, q]
            out[h, q, :, 16:24] = picked[q, h]


def advance_kernel(received, states, gain, new_states, fetched):
    factor = gain[...]
    carried = states[0]
    for s in range(received.shape[0]):
        fine = received[s, :, 0:16]
        change = fine - factor * states[s]
        carried = factor * carried + change
        new_states[s] = carried
        tile = received[s, :, 16:24]
        fetched[s, 0] = tile[:, 0:4]
        fetched[s, 1] = tile[:, 4:8]


def exchange(value, axes):
    return lax.all_to_all(value, axes, 0, 0, tiled=True)


def call(kernel, name, shapes, kinds, scratch=(), **more):
    outs = [jax.ShapeDtypeStruct(shape, jnp.float32) for shape in shapes]
    return pl.pallas_call(
        kernel,
        out_shape=outs,
        in_specs=kinds,
        out_specs=[VMEM] * len(outs),
        scratch_shapes=[pltpu.VMEM(shape, jnp.float32) for shape in scratch],
        compiler_params=PARAMS,
        name=name,
        **more,
    )


def body(states, diffusivity, coarse_gain, read_block, read_count):
    slices, thick, own_rows, lanes = states.shape
    y = lax.axis_index("y")
    x = lax.axis_index("x")
    ny, nx = lax.axis_size("y"), lax.axis_size("x")
    me = lax.axis_index(RING)
    cut = lax.axis_index(CUTS)
    tile_rows = 2 * own_rows
    wide = tile_rows + 2 * FINE
    half = slices // 2
    x_up = [(i, i + 1) for i in range(nx - 1)]
    x_down = [(i + 1, i) for i in range(nx - 1)]

    y_up = [(i, i + 1) for i in range(ny - 1)]
    y_down = [(i + 1, i) for i in range(ny - 1)]

    window = y * tile_rows - FINE + lax.axis_index("zh") * (wide // 2)
    inside = jnp.clip(window, 0, diffusivity.shape[1] - wide // 2)
    kappa = lax.dynamic_slice_in_dim(diffusivity, inside, wide // 2, 1)
    layers = thick * own_rows
    packed = layers + wide // 2
    (load,) = call(
        load_kernel, "load", [(slices, packed, lanes)], [SMEM, VMEM, VMEM]
    )((window - inside)[None], states, kappa)
    own = exchange(load, RING).reshape(2, half, packed, lanes)
    ends_of = own[:, :, :layers].reshape(2, half, thick, own_rows, lanes)
    south = lax.ppermute(ends_of[1, :, :, own_rows - FINE :], "y", y_up)
    north = lax.ppermute(ends_of[0, :, :, :FINE], "y", y_down)
    part = (FINE, wide, lanes)
    mine = own[:, :, layers:]
    other = lax.ppermute(mine, "c", [(0, 1), (1, 0)])
    kappas, k_first, k_second = call(
        gather_kernel,
        "gather",
        [(2 * FINE, wide, lanes), part, part],
        [SMEM, VMEM, VMEM],
        [(2 * FINE, wide, lanes)],
    )(lax.axis_index("c")[None], mine, other)
    k_low = lax.ppermute(k_second, "x", x_up)
    k_high = lax.ppermute(k_first, "x", x_down)
    first, second = call(join_kernel, "join", [part] * 2, [VMEM] * 3)(own, south, north)
    low = lax.ppermute(second, "x", x_up)
    high = lax.ppermute(first, "x", x_down)

    flags = [y > 0, y < ny - 1, x > 0, x < nx - 1]
    edge = jnp.stack([flag.astype(jnp.int32) for flag in flags])
    deep = half * thick
    region = (deep + 2 * FINE, wide, lanes)
    coefficients = call(
        coefficient_kernel, "coefficients", [region] * 7, [SMEM] + [VMEM] * 3
    )(edge, k_low, kappas, k_high)
    (kept,) = call(
        inner_kernel, "inner", [(FINE - 1, 4, *part[1:])], [VMEM] * 9, [(deep, *part[1:])]
    )(first, second, *coefficients)
    fine, ends = call(
        fine_kernel,
        "fine",
        [(ny, deep // ny, tile_rows, lanes), (2, half, thick, own_rows, lanes)],
        [VMEM] * 12,
        [region],
    )(low, first, second, high, kept, *coefficients)

    tiles = exchange(fine, "y")
    (picked,) = call(
        pick_kernel,
        "pick",
        [(slices, thick, 2 * BY, lanes)],
        [SMEM, SMEM, SMEM, VMEM],
    )(read_block.reshape(-1), read_count.reshape(-1), me[None], tiles)
    picked = exchange(picked, "y").reshape(ny, 2, thick, 2 * BY, lanes)
    (payload,) = call(
        pack_kernel, "pack", [(2, half, thick, own_rows + 2 * BY, lanes)], [VMEM] * 2
    )(ends, picked)
    received = exchange(
        payload.reshape(slices, thick, own_rows + 2 * BY, lanes), RING
    )
    gain = lax.dynamic_slice_in_dim(coarse_gain, cut * own_rows, own_rows, 1)
    new_states, fetched = call(
        advance_kernel,
        "advance",
        [states.shape, (slices, 2, thick, BY, lanes)],
        [VMEM] * 3,
    )(received, states, gain)
    return new_states, fetched[None]


def solution(mesh):
    grid = Mesh(mesh.devices.reshape(8, 2, 4, 4, 2), ("y", "zh", "x", "zl", "c"))
    placed = (P(None, SLAB, CUTS, None), P(SLAB, None, None), P(SLAB, None, None), P(), P())
    return jax.shard_map(
        body,
        mesh=grid,
        in_specs=placed,
        out_specs=(P(None, SLAB, CUTS, None), P(CUTS, None, None, SLAB, None, None)),
        check_vma=False,
    )
```

```python
import jax
import jax.numpy as jnp
from jax import lax
from jax.experimental import pallas as pl
from jax.experimental.pallas import tpu as pltpu
from jax.sharding import Mesh
from jax.sharding import PartitionSpec as P

FINE = 8
BY = 4
COURANT = 0.45

RING = ("zh", "zl", "c")
SLAB = ("x", "zl", "c")
CUTS = ("y", "zh")

VMEM = pl.BlockSpec(memory_space=pltpu.VMEM)
SMEM = pl.BlockSpec(memory_space=pltpu.SMEM)
PARAMS = pltpu.CompilerParams(vmem_limit_bytes=40 * 2**20)


def load_kernel(states, kappa, out):
    for d in range(out.shape[0]):
        for k in range(2):
            out[d, 16 * k : 16 * k + 16] = states[d, k]
        out[d, 32:56] = kappa[d % 2]


def gather_kernel(place, mine, other, own, first, second, kappa):
    for part, source in ((place[0], mine), (1 - place[0], other)):
        for j in range(8):
            for h in range(2):
                kappa[2 * j + part, 24 * h : 24 * h + 24] = source[h, j]
    for z in range(FINE):
        own[z] = first[z] = kappa[z]
        own[FINE + z] = second[z] = kappa[FINE + z]


def join_kernel(own, south, north, first, second):
    for out, start in ((first, 0), (second, 4)):
        for j in range(4):
            for k in range(2):
                layer = 2 * j + k
                out[layer, 0:8] = south[start + j, k]
                out[layer, 8:24] = own[0, start + j, 16 * k : 16 * k + 16]
                out[layer, 24:40] = own[1, start + j, 16 * k : 16 * k + 16]
                out[layer, 40:48] = north[start + j, k]


def coefficient_kernel(
    edge, low, own, high, c0, zp, zm, yp, ym, xp, xm
):
    depth, rows, lanes = c0.shape

    def at(z):
        return low[z] if z < 8 else own[z - 8] if z < 24 else high[z - 24]

    row = lax.broadcasted_iota(jnp.int32, (rows, lanes), 0)
    lane = lax.broadcasted_iota(jnp.int32, (rows, lanes), 1)
    inside = jnp.where(
        row < 8, edge[0], jnp.where(row >= rows - 8, edge[1], 1)
    ).astype(jnp.float32)
    below = inside * edge[2].astype(jnp.float32)
    above = inside * edge[3].astype(jnp.float32)
    not_first = jnp.where(lane == 0, 0.0, 1.0)
    not_last = jnp.where(lane == lanes - 1, 0.0, 1.0)
    down, here = 0.5 * (at(0) + at(1)), at(1)
    for z in range(1, depth - 1):
        mask = below if z < 8 else above if z >= depth - 8 else inside
        after = at(z + 1)
        up = 0.5 * (here + after)
        north = 0.5 * (here + pltpu.roll(here, rows - 1, 0))
        south = 0.5 * (here + pltpu.roll(here, 1, 0))
        east = 0.5 * (here + pltpu.roll(here, lanes - 1, 1) * not_last)
        west = 0.5 * (here + pltpu.roll(here, 1, 1) * not_first)
        total = ((up + down) + (north + south)) + (east + west)
        c0[z] = ((1.0 - COURANT) - total) * mask
        zp[z] = up * mask
        zm[z] = (down + COURANT) * mask
        yp[z] = north * mask
        ym[z] = south * mask
        xp[z] = east * (mask * not_last)
        xm[z] = west * (mask * not_first)
        down, here = up, after


def advance_layer(coefficients, z, below, here, above):
    c0, zp, zm, yp, ym, xp, xm = coefficients
    rows, lanes = here.shape
    return (
        (c0[z] * here + zp[z] * above)
        + (zm[z] * below + yp[z] * pltpu.roll(here, rows - 1, 0))
        + (ym[z] * pltpu.roll(here, 1, 0) + xp[z] * pltpu.roll(here, lanes - 1, 1))
        + xm[z] * pltpu.roll(here, 1, 1)
    )


def inner_kernel(first, second, *refs):
    *coefficients, kept, u = refs
    for step in range(1, FINE):

        def at(z):
            if step == 1:
                return first[z - 8] if z < 16 else second[z - 16]
            return u[z - 8]

        lowest, end = 8 + step, 24 - step
        below, here = at(lowest - 1), at(lowest)
        for z in range(lowest, end):
            above = at(z + 1)
            new = advance_layer(coefficients, z, below, here, above)
            u[z - 8] = new
            if z < lowest + 2:
                kept[step - 1, z - lowest] = new
            if z >= end - 2:
                kept[step - 1, 4 + z - end] = new
            below, here = here, above


def fine_kernel(low, first, second, high, kept, *refs):
    *coefficients, out, ends, u = refs
    rows = low.shape[1]
    parts = (low, first, second, high)
    for step in range(1, FINE + 1):
        done = step - 1

        def at(z):
            if done == 0:
                return parts[z // 8][z % 8]
            if z < 8 + done or z >= 24 - done:
                return u[z]
            return kept[done - 1, z - 8 - done if z < 16 else 4 + z - 24 + done]

        for start in (step, 24 - step):
            below, here = at(start - 1), at(start)
            for z in range(start, start + 8):
                above = at(z + 1)
                new = advance_layer(coefficients, z, below, here, above)
                if step < FINE:
                    u[z] = new
                else:
                    q, k = (z - 8) // 2, z % 2
                    out[q, k] = new[8 : rows - 8]
                    ends[0, q, k] = new[8:24]
                    ends[1, q, k] = new[24:40]
                below, here = here, above


def pick_kernel(blocks, counts, me, tiles, out):
    slices = out.shape[0]
    upper = lax.broadcasted_iota(jnp.int32, out.shape[2:], 0) >= BY
    for d in range(slices):
        count = counts[d * slices + me[0]]
        first = blocks[(d * slices + me[0]) * 2]
        second = blocks[(d * slices + me[0]) * 2 + 1]
        for k in range(2):
            def half(block, slot):
                start = pl.multiple_of(((block >> 1) & 3) * 8, 8)
                tile = tiles[(block >> 3) & 7, k, pl.ds(start, 8), :]
                turned = pltpu.roll(tile, BY, 0)
                fits = jnp.where((block & 1) == slot, 1, 0)
                live = jnp.where(slot < count, 1, 0)
                chosen = jnp.where(jnp.full(tile.shape, fits) == 1, tile, turned)
                return jnp.where(jnp.full(tile.shape, live) == 1, chosen, 0.0)

            out[d, k] = jnp.where(upper, half(second, 1), half(first, 0))


def pack_kernel(ends, picked, out):
    for h in range(2):
        for q in range(8):
            out[h, q, :, 0:16] = ends[h, q]
            out[h, q, :, 16:24] = picked[q, h]


def advance_kernel(received, states, gain, new_states, fetched):
    factor = gain[...]
    carried = states[0]
    for s in range(received.shape[0]):
        fine = received[s, :, 0:16]
        change = fine - factor * states[s]
        carried = factor * carried + change
        new_states[s] = carried
        tile = received[s, :, 16:24]
        fetched[s, 0] = tile[:, 0:4]
        fetched[s, 1] = tile[:, 4:8]


def exchange(value, axes):
    return lax.all_to_all(value, axes, 0, 0, tiled=True)


def call(kernel, name, shapes, kinds, scratch=(), **more):
    outs = [jax.ShapeDtypeStruct(shape, jnp.float32) for shape in shapes]
    return pl.pallas_call(
        kernel,
        out_shape=outs,
        in_specs=kinds,
        out_specs=[VMEM] * len(outs),
        scratch_shapes=[pltpu.VMEM(shape, jnp.float32) for shape in scratch],
        compiler_params=PARAMS,
        name=name,
        **more,
    )


def body(states, diffusivity, coarse_gain, read_block, read_count):
    slices, thick, own_rows, lanes = states.shape
    y = lax.axis_index("y")
    x = lax.axis_index("x")
    ny, nx = lax.axis_size("y"), lax.axis_size("x")
    me = lax.axis_index(RING)
    cut = lax.axis_index(CUTS)
    tile_rows = 2 * own_rows
    wide = tile_rows + 2 * FINE
    half = slices // 2
    x_up = [(i, i + 1) for i in range(nx - 1)]
    x_down = [(i + 1, i) for i in range(nx - 1)]

    y_up = [(i, i + 1) for i in range(ny - 1)]
    y_down = [(i + 1, i) for i in range(ny - 1)]

    padded = jnp.pad(diffusivity, ((0, 0), (FINE, FINE), (0, 0)))
    window = y * tile_rows + lax.axis_index("zh") * (wide // 2)
    kappa = lax.dynamic_slice_in_dim(padded, window, wide // 2, 1)
    layers = thick * own_rows
    packed = layers + wide // 2
    (load,) = call(
        load_kernel, "load", [(slices, packed, lanes)], [VMEM] * 2
    )(states, kappa)
    own = exchange(load, RING).reshape(2, half, packed, lanes)
    upper = [own[1, :, r - FINE : r] for r in (own_rows, 2 * own_rows)]
    lower = [own[0, :, r : r + FINE] for r in (0, own_rows)]
    south = lax.ppermute(jnp.stack(upper, axis=1), "y", y_up)
    north = lax.ppermute(jnp.stack(lower, axis=1), "y", y_down)
    part = (FINE, wide, lanes)
    mine = own[:, :, layers:]
    other = lax.ppermute(mine, "c", [(0, 1), (1, 0)])
    kappas, k_first, k_second = call(
        gather_kernel,
        "gather",
        [(2 * FINE, wide, lanes), part, part],
        [SMEM, VMEM, VMEM],
        [(2 * FINE, wide, lanes)],
    )(lax.axis_index("c")[None], mine, other)
    k_low = lax.ppermute(k_second, "x", x_up)
    k_high = lax.ppermute(k_first, "x", x_down)
    first, second = call(join_kernel, "join", [part] * 2, [VMEM] * 3)(own, south, north)
    low = lax.ppermute(second, "x", x_up)
    high = lax.ppermute(first, "x", x_down)

    flags = [y > 0, y < ny - 1, x > 0, x < nx - 1]
    edge = jnp.stack([flag.astype(jnp.int32) for flag in flags])
    deep = half * thick
    region = (deep + 2 * FINE, wide, lanes)
    coefficients = call(
        coefficient_kernel, "coefficients", [region] * 7, [SMEM] + [VMEM] * 3
    )(edge, k_low, kappas, k_high)
    (kept,) = call(
        inner_kernel, "inner", [(FINE - 1, 4, *part[1:])], [VMEM] * 9, [(deep, *part[1:])]
    )(first, second, *coefficients)
    fine, ends = call(
        fine_kernel,
        "fine",
        [(ny, deep // ny, tile_rows, lanes), (2, half, thick, own_rows, lanes)],
        [VMEM] * 12,
        [region],
    )(low, first, second, high, kept, *coefficients)

    tiles = exchange(fine, "y")
    (picked,) = call(
        pick_kernel,
        "pick",
        [(slices, thick, 2 * BY, lanes)],
        [SMEM, SMEM, SMEM, VMEM],
    )(read_block.reshape(-1), read_count.reshape(-1), me[None], tiles)
    picked = exchange(picked, "y").reshape(ny, 2, thick, 2 * BY, lanes)
    (payload,) = call(
        pack_kernel, "pack", [(2, half, thick, own_rows + 2 * BY, lanes)], [VMEM] * 2
    )(ends, picked)
    received = exchange(
        payload.reshape(slices, thick, own_rows + 2 * BY, lanes), RING
    )
    gain = lax.dynamic_slice_in_dim(coarse_gain, cut * own_rows, own_rows, 1)
    new_states, fetched = call(
        advance_kernel,
        "advance",
        [states.shape, (slices, 2, thick, BY, lanes)],
        [VMEM] * 3,
    )(received, states, gain)
    return new_states, fetched[None]


def solution(mesh):
    grid = Mesh(mesh.devices.reshape(8, 2, 4, 4, 2), ("y", "zh", "x", "zl", "c"))
    placed = (P(None, SLAB, CUTS, None), P(SLAB, None, None), P(SLAB, None, None), P(), P())
    return jax.shard_map(
        body,
        mesh=grid,
        in_specs=placed,
        out_specs=(P(None, SLAB, CUTS, None), P(CUTS, None, None, SLAB, None, None)),
        check_vma=False,
    )
```
